32 devices in a mesh: gx: 8 (over z, x), gy: 2 (over y), gz: 2 (over core).
Axes of the slice: x: 2, y: 2, z: 4, core: 2. Of those that a mesh axis runs over, the one named last changes fastest.
Arguments:
- state_field: float32 [128, 5, 32, 256], P('gx', None, 'gy', 'gz'), may hold values from -6 to 6
- source: float32 [128, 5, 32, 256], P('gx', None, 'gy', 'gz'), may hold values from -6 to 6
- fluid_mask: int32 [128, 32, 256], P('gx', 'gy', 'gz'), may hold values 0 or 1
- cell_kind: int32 [128, 32, 256], P('gx', 'gy', 'gz'), may hold values from 0 to 2
- boundary_side_number: int32 [128, 32, 256], P('gx', 'gy', 'gz'), may hold values from 0 to 11
- center_matrix: float32 [5, 5], replicated, may hold values from -2.5 to 2.5
- flux_jacobian_blocks: float32 [6, 5, 5], replicated, may hold values from -1 to 1
- wall_matrix: float32 [5, 5], replicated, may hold values from -2.5 to 2.5
- diag_inverse: float32 [128, 5, 5, 32, 256], P('gx', None, None, 'gy', 'gz'), may hold values from -0.01 to 0.1
- lower_coupling: float32 [5, 5], replicated, may hold values from -10 to 10
- upper_neighbour_block: float32 [5, 5], replicated, may hold values from -10 to 10
Outputs:
- update: float32 [128, 5, 32, 256], P('gx', None, 'gy', 'gz')
- residual: float32 [128, 5, 32, 256], P('gx', None, 'gy', 'gz')
The draws below stay inside these ranges and needn't reach their ends.
Inputs may be any that keep to these rules, and one draw needn't show every extreme that they name: `boundary_side_number`: values 0 to 5 name the face of a cell that is a wall (lower x, upper x, lower y, upper y, lower z, upper z); 6 or more: no wall face. `cell_kind`: 0 full cell, 1 cut cell, 2 small cut cell.
All inputs are finite; a program needn't handle non-finite values. No bound on the sum of `fluid_mask` on one device may be relied on, other than what follows from the above.
Results may differ from the reference program's by a relative error of at most 0.00018.
Values sent between devices are 32-bit elements; how exact they have to be, the bound alone decides.
No kernel may reach another device: no remote copies, remote signals or barrier semaphores. Data moves between devices by JAX's collectives and lax.ppermute only.
A program may use at most 64 MiB of HBM per device.

```python
import jax
import jax.numpy as jnp
from jax import lax

COMP = 5
MESH_SPAN_EAST = 128
NY = 32
NZ = 256


def draw_diag_inverse(key, part):
    key_jitter = jax.random.fold_in(key, 11)
    seed_position = jax.random.fold_in(key, 12)
    key_depth = jax.random.fold_in(key, 13)
    jitter = jnp.clip(0.03 * jax.random.normal(key_jitter, (MESH_SPAN_EAST, 5, 5, NY, NZ), jnp.float32), -0.1, 0.1)
    packet_bundles = jax.random.randint(seed_position, (3,), 0, MESH_SPAN_EAST)
    nesting_tiers = jax.random.uniform(key_depth, (3,), jnp.float32, 0.6, 0.85)
    vertical_strip = jnp.arange(MESH_SPAN_EAST)
    magnitude_multiplier = jnp.prod(jnp.where(vertical_strip[:, None] == packet_bundles[None, :], nesting_tiers[None, :], 1.0), axis=1)
    identity = jnp.eye(5, dtype=jnp.float32)
    offdiag = jitter * (1.0 - identity)[None, :, :, None, None]
    return 0.1 * (identity[None, :, :, None, None] * magnitude_multiplier[:, None, None, None, None] + offdiag)


def plane_rotation(size, first, second, angle):
    identity = jnp.eye(size, dtype=jnp.float32)
    cosine = jnp.cos(angle)
    sine = jnp.sin(angle)
    rotation = identity.at[first, first].set(cosine).at[second, second].set(cosine)
    rotation = rotation.at[first, second].set(-sine).at[second, first].set(sine)
    return rotation


def coupling_matrix(key):
    key_rates = jax.random.fold_in(key, 21)
    key_angles = jax.random.fold_in(key, 22)
    key_signs = jax.random.fold_in(key, 23)
    rates = jax.random.uniform(key_rates, (5,), jnp.float32, 1.0, 2.0)
    keeping = jnp.exp(-rates / MESH_SPAN_EAST).astype(jnp.float32)
    magnitudes = jax.random.uniform(key_angles, (5,), jnp.float32, 0.2, 0.5)
    signs = jnp.where(jax.random.uniform(key_signs, (5,), jnp.float32) < 0.5, -1.0, 1.0)
    angles = magnitudes * signs
    planes = [(0, 1), (2, 3), (1, 2), (3, 4), (0, 4)]
    rotation = jnp.eye(5, dtype=jnp.float32)
    for position in range(5):
        first, second = planes[position]
        turned = plane_rotation(5, first, second, angles[position])
        rotation = jnp.dot(turned, rotation, precision=lax.Precision.HIGHEST)
    return keeping[:, None] * rotation / 0.1


def draw_lower_coupling(key, part):
    return coupling_matrix(jax.random.fold_in(key, 31))


def draw_upper_neighbour_block(key, part):
    return coupling_matrix(jax.random.fold_in(key, 32))


def plant(result, key, smallest, top_value):
    longest = result.shape.index(max(result.shape))
    spots = []
    for shift in (0, 1):
        where = [jax.random.randint(jax.random.fold_in(key, axis), (), 0, length) for axis, length in enumerate(result.shape)]
        where[longest] = (where[longest] + shift) % result.shape[longest]
        spots.append(tuple(where))
    return result.at[spots[0]].set(smallest).at[spots[1]].set(top_value)


def steps_of(stream_key, extent, split, low, top_value):
    level, own = 1.0, jax.random.fold_in(stream_key, 6)
    for dim, blocks in split:
        heights = jnp.exp(jax.random.uniform(jax.random.fold_in(own, dim), (blocks,), jnp.float32, low / len(split), top_value / len(split)))
        level = level * jnp.repeat(heights, extent[dim] // blocks).reshape([-1 if axis == dim else 1 for axis in range(len(extent))])
    return level


def gaussian(stream_key, shape, scale, limit, split=(), held_as=jnp.bfloat16):
    drawn = scale * jax.random.normal(stream_key, shape, jnp.float32)
    if split:
        drawn = drawn * steps_of(stream_key, shape, split, -0.22, 0.18)
    return jnp.clip(drawn, -limit, limit).astype(held_as)


def setup_inputs(seed: int = 0) -> dict:
    key_of = jax.random.split(jax.random.key(seed), 12)
    state_field = gaussian(key_of[0], (MESH_SPAN_EAST, COMP, NY, NZ), 1.0, 6.0, ((0, 8), (2, 2), (3, 2)), jnp.float32)
    source = gaussian(key_of[1], (MESH_SPAN_EAST, COMP, NY, NZ), 1.0, 6.0, ((0, 8), (2, 2), (3, 2)), jnp.float32)
    fluid_mask = plant((jax.random.randint(key_of[2], (MESH_SPAN_EAST, NY, NZ), 0, 16) < 15).astype(jnp.int32), jax.random.fold_in(key_of[2], 1), 0, 1)
    cell_kind = plant(jax.random.randint(key_of[3], (MESH_SPAN_EAST, NY, NZ), 0, 3), jax.random.fold_in(key_of[3], 1), 0, 2).astype(jnp.int32)
    boundary_side_number = plant(jax.random.randint(key_of[4], (MESH_SPAN_EAST, NY, NZ), 0, 12), jax.random.fold_in(key_of[4], 1), 0, 11).astype(jnp.int32)
    center_matrix = gaussian(key_of[5], (COMP, COMP), COMP ** -0.5, 2.5, (), jnp.float32)
    flux_jacobian_blocks = gaussian(key_of[6], (6, COMP, COMP), 0.2, 1.0, (), jnp.float32)
    wall_matrix = gaussian(key_of[7], (COMP, COMP), COMP ** -0.5, 2.5, (), jnp.float32)
    diag_inverse = draw_diag_inverse(jax.random.fold_in(key_of[11], 71), 0)
    lower_coupling = draw_lower_coupling(jax.random.fold_in(key_of[11], 71), 0)
    upper_neighbour_block = draw_upper_neighbour_block(jax.random.fold_in(key_of[11], 71), 0)
    return dict(state_field=state_field, source=source, fluid_mask=fluid_mask, cell_kind=cell_kind, boundary_side_number=boundary_side_number, center_matrix=center_matrix, flux_jacobian_blocks=flux_jacobian_blocks, wall_matrix=wall_matrix, diag_inverse=diag_inverse, lower_coupling=lower_coupling, upper_neighbour_block=upper_neighbour_block)


def const_apply(matrix, vector):
    return jnp.einsum("ab,...byz->...ayz", matrix, vector, precision=lax.Precision.HIGHEST)


def volume_operator(blocks, vector):
    return jnp.sum(blocks * vector[..., None, :, :, :], axis=-3)


def flux_residual(state_field, padded, source, fluid, cell_kind, boundary_side_number, center_matrix, flux_jacobian_blocks, wall_matrix):
    neighbours = [padded[:-2, :, 1:-1, 1:-1], padded[2:, :, 1:-1, 1:-1],
                  padded[1:-1, :, :-2, 1:-1], padded[1:-1, :, 2:, 1:-1],
                  padded[1:-1, :, 1:-1, :-2], padded[1:-1, :, 1:-1, 2:]]
    walled = const_apply(wall_matrix, state_field)
    flux = const_apply(center_matrix, state_field)
    for facing in range(6):
        at_wall = (boundary_side_number == facing)[:, None]
        flux = flux + jnp.where(at_wall, walled, const_apply(flux_jacobian_blocks[facing], neighbours[facing]))
    weight = jnp.where(cell_kind == 0, 1.0, jnp.where(cell_kind == 1, 2.0, 4.0)).astype(jnp.float32)
    return fluid[:, None] * (source - flux) * weight[:, None]


def reference(state_field, source, fluid_mask, cell_kind, boundary_side_number, center_matrix, flux_jacobian_blocks, wall_matrix, diag_inverse, lower_coupling, upper_neighbour_block):
    fluid = fluid_mask.astype(jnp.float32)
    masked = state_field * fluid[:, None]
    padded = jnp.pad(masked, ((1, 1), (0, 0), (1, 1), (1, 1)))
    residual = flux_residual(state_field, padded, source, fluid, cell_kind, boundary_side_number, center_matrix, flux_jacobian_blocks, wall_matrix)

    def forward(carry, inputs):
        blocks, term = inputs
        carry = volume_operator(blocks, term + const_apply(lower_coupling, carry))
        return carry, carry

    def backward(carry, inputs):
        blocks, value = inputs
        carry = value - volume_operator(blocks, const_apply(upper_neighbour_block, carry))
        return carry, carry

    zeroed = jnp.zeros((COMP, NY, NZ), jnp.float32)
    final, swept = lax.scan(forward, zeroed, (diag_inverse, residual))
    final, update = lax.scan(backward, zeroed, (diag_inverse, swept), reverse=True)
    return update, residual
```

```python
import functools

import jax
import jax.numpy as jnp
from jax import lax
from jax.experimental import pallas as pl
from jax.experimental.pallas import tpu as pltpu
from jax.sharding import PartitionSpec as P

SUB = 8
LANES = 128
MIB = 1 << 20
SHRINK = 2.0**-24
GROW = 2.0**24


def round_up(value, unit):
    return -(-value // unit) * unit


class Sizes:
    def __init__(self, state_shape):
        self.nx, self.comps, self.ny, self.nz = state_shape
        self.parts = lax.axis_size("gx")
        self.vregs = self.ny // SUB
        self.rows = self.ny // self.parts
        assert self.nz == LANES and self.parts % SUB == 0
        assert self.ny % self.parts == 0
        self.square = self.comps * self.comps
        self.map_rows = round_up(3 * self.square * self.rows, SUB)
        self.vec_rows = round_up(2 * self.comps * self.rows, SUB)
        self.edge_count = self.nx * self.comps * self.vregs
        self.edge_rows = SUB * -(-self.edge_count // LANES)

    def start(self, index, vreg, chunk):
        first = vreg * SUB
        return (first % self.parts) * chunk + index * self.rows + first // self.parts


def scatter(sizes, ref, chunk, index, value):
    for vreg in range(sizes.vregs):
        start = sizes.start(index, vreg, chunk)
        ref[pl.ds(start, SUB, stride=chunk), :] = value[vreg * SUB : (vreg + 1) * SUB]


def gather(sizes, ref, chunk, index):
    parts = []
    for vreg in range(sizes.vregs):
        start = sizes.start(index, vreg, chunk)
        parts.append(ref[pl.ds(start, SUB, stride=chunk), :])
    return jnp.concatenate(parts, axis=0)


def combine(terms):
    terms = list(terms)
    while len(terms) > 1:
        terms = [
            terms[i] + terms[i + 1] if i + 1 < len(terms) else terms[i]
            for i in range(0, len(terms), 2)
        ]
    return terms[0]


def maps_kernel(sizes, diag_ref, lower_ref, upper_ref, out_ref, fwd_ref, back_ref, mix_ref):
    comps, nx = sizes.comps, sizes.nx
    span = range(comps)

    def product(x, coupling_ref, negate):
        sign = -1.0 if negate else 1.0
        scale = [[sign * coupling_ref[b, c] for c in span] for b in span]
        rows = []
        for a in span:
            diag = [diag_ref[x, a, b] for b in span]
            rows.append([combine(diag[b] * scale[b][c] for b in span) for c in span])
        return rows

    first = product(0, lower_ref, False)
    for a in span:
        for c in span:
            fwd_ref[0, a, c] = first[a][c] * SHRINK

    def forward(x, carry):
        step = product(x, lower_ref, False)
        for d in span:
            column = [fwd_ref[x - 1, c, d] for c in span]
            for a in span:
                fwd_ref[x, a, d] = combine(step[a][c] * column[c] for c in span)
        return carry

    lax.fori_loop(1, nx, forward, 0)

    last = product(nx - 1, upper_ref, True)
    for a in span:
        for d in span:
            back_ref[(nx - 1) % 2, a, d] = last[a][d]
            mix_ref[(nx - 1) % 2, a, d] = fwd_ref[nx - 1, a, d]

    def backward(count, carry):
        x = nx - 1 - count
        now, before = lax.rem(x, 2), lax.rem(x + 1, 2)
        step = product(x, upper_ref, True)
        for d in span:
            column = [back_ref[before, c, d] for c in span]
            for a in span:
                back_ref[now, a, d] = combine(step[a][c] * column[c] for c in span)
        for d in span:
            column = [mix_ref[before, c, d] for c in span]
            for a in span:
                mix_ref[now, a, d] = fwd_ref[x, a, d] + combine(
                    step[a][c] * column[c] for c in span
                )
        return carry

    lax.fori_loop(1, nx, backward, 0)

    for a in span:
        for d in span:
            index = a * comps + d
            scatter(sizes, out_ref, sizes.map_rows, index, fwd_ref[nx - 1, a, d] * GROW)
            scatter(sizes, out_ref, sizes.map_rows, sizes.square + index, back_ref[0, a, d])
            scatter(sizes, out_ref, sizes.map_rows, 2 * sizes.square + index, mix_ref[0, a, d])


def edges_kernel(sizes, gy_two, gz_two, state_ref, mask_ref, *refs):
    masked_ref, west_ref, east_ref, *rest = refs
    y_refs = rest[: 1 if gy_two else 2]
    z_refs = rest[len(y_refs) :]
    nx, comps = sizes.nx, sizes.comps
    lane = lax.broadcasted_iota(jnp.int32, (SUB, LANES), 1)
    low_z = (lax.axis_index("gz") == 0).astype(jnp.int32)
    shifts = [low_z] if gz_two else [0, 1]
    packed = [[jnp.zeros((SUB, LANES), jnp.float32)] * (sizes.edge_rows // SUB) for _ in shifts]
    low_y = lax.axis_index("gy") == 0
    for x in range(nx):
        fluid = mask_ref[x].astype(jnp.float32)
        for c in range(comps):
            value = state_ref[x, c] * fluid
            masked_ref[x, c] = value
            if x == 0:
                west_ref[c] = value
            if x == nx - 1:
                east_ref[c] = value
            row = pl.ds(x * comps + c, 1)
            bottom, top = value[0:1], value[sizes.ny - 1 : sizes.ny]
            if gy_two:
                y_refs[0][row, :] = jnp.where(low_y, top, bottom)
            else:
                y_refs[0][row, :] = bottom
                y_refs[1][row, :] = top
            for v in range(sizes.vregs):
                index = (x * comps + c) * sizes.vregs + v
                group, place = divmod(index, LANES)
                part = value[v * SUB : (v + 1) * SUB]
                for side, shift in enumerate(shifts):
                    turned = pltpu.roll(part, lax.rem(jnp.int32(place) + shift, LANES), 1)
                    packed[side][group] = jnp.where(lane == place, turned, packed[side][group])
    for side in range(len(shifts)):
        for group, value in enumerate(packed[side]):
            z_refs[side][group * SUB : (group + 1) * SUB, :] = value


def sweep_steps(sizes, diag_ref, lower_ref, upper_ref):
    span = range(sizes.comps)

    def apply(x, vector):
        return [combine(diag_ref[x, a, b] * vector[b] for b in span) for a in span]

    def coupled(matrix_ref, vector):
        return [combine(matrix_ref[a, b] * vector[b] for b in span) for a in span]

    def forward(x, term, carry):
        pushed = coupled(lower_ref, carry)
        return apply(x, [term[a] + pushed[a] for a in span])

    def backward(x, value, carry):
        pulled = apply(x, coupled(upper_ref, carry))
        return [value[a] - pulled[a] for a in span]

    return forward, backward


def residual_kernel(
    sizes, gy_two, gz_two,
    state_ref, masked_ref, source_ref, mask_ref, kind_ref, side_ref,
    center_ref, flux_ref, wall_ref, diag_ref, lower_ref, upper_ref,
    west_ref, east_ref, south_ref, north_ref, below_ref, above_ref,
    residual_ref, out_ref, swept_ref, zlow_ref, zhigh_ref,
):
    nx, comps, ny = sizes.nx, sizes.comps, sizes.ny
    span = range(comps)
    shape = (ny, LANES)
    lane = lax.broadcasted_iota(jnp.int32, (SUB, LANES), 1)
    row_index = lax.broadcasted_iota(jnp.int32, shape, 0)
    full_lane = lax.broadcasted_iota(jnp.int32, shape, 1)
    low_y = lax.axis_index("gy") == 0
    low_z = lax.axis_index("gz") == 0
    below, above = below_ref[...], above_ref[...]
    if gz_two:
        below = jnp.where(low_z, 0.0, below)
        above = jnp.where(low_z, above, 0.0)
    zlow_ref[...] = below
    zhigh_ref[...] = above
    forward, backward = sweep_steps(sizes, diag_ref, lower_ref, upper_ref)

    def edge_column(ref, x, c, target):
        parts = []
        for v in range(sizes.vregs):
            index = (x * comps + c) * sizes.vregs + v
            group = pl.multiple_of((index // LANES) * SUB, SUB)
            shift = lax.rem(target + LANES - lax.rem(index, LANES), LANES)
            parts.append(pltpu.roll(ref[pl.ds(group, SUB), :], shift, 1))
        return jnp.concatenate(parts, axis=0)

    def plane(x, carry):
        side = side_ref[x]
        fluid = mask_ref[x].astype(jnp.float32)
        kind = kind_ref[x]
        weight = fluid * jnp.where(kind == 0, 1.0, jnp.where(kind == 1, 2.0, 4.0))
        walled = side < 6
        open_face = [side != d for d in range(6)]
        total = [None] * comps

        def add(get, c, value):
            for a in span:
                term = get(a, c) * value
                total[a] = term if total[a] is None else total[a] + term

        for c in span:
            value = state_ref[x, c]
            add(lambda a, b: center_ref[a, b], c, value)
            add(lambda a, b: wall_ref[a, b], c, jnp.where(walled, value, 0.0))
            masked = masked_ref[x, c]
            row = pl.ds(x * comps + c, 1)
            south = jnp.broadcast_to(south_ref[row, :], shape)
            north = jnp.broadcast_to(north_ref[row, :], shape)
            if gy_two:
                south = jnp.where(low_y, 0.0, south)
                north = jnp.where(low_y, north, 0.0)
            neighbours = [
                jnp.where(x == 0, west_ref[c], masked_ref[jnp.maximum(x - 1, 0), c]),
                jnp.where(x == nx - 1, east_ref[c], masked_ref[jnp.minimum(x + 1, nx - 1), c]),
                jnp.where(row_index == 0, south, pltpu.roll(masked, 1, 0)),
                jnp.where(row_index == ny - 1, north, pltpu.roll(masked, ny - 1, 0)),
                jnp.where(full_lane == 0, edge_column(zlow_ref, x, c, 0), pltpu.roll(masked, 1, 1)),
                jnp.where(
                    full_lane == LANES - 1,
                    edge_column(zhigh_ref, x, c, LANES - 1),
                    pltpu.roll(masked, LANES - 1, 1),
                ),
            ]
            for d in range(6):
                add(
                    functools.partial(lambda e, a, b: flux_ref[e, a, b], d),
                    c,
                    jnp.where(open_face[d], neighbours[d], 0.0),
                )
        term = [weight * (source_ref[x, a] - total[a]) for a in span]
        for a in span:
            residual_ref[x, a] = term[a]
        carry = forward(x, term, carry)
        for a in span:
            swept_ref[x, a] = carry[a]
        return tuple(carry)

    zeroed = tuple(jnp.zeros(shape, jnp.float32) for _ in span)
    carry = lax.fori_loop(0, nx, plane, zeroed)
    for a in span:
        scatter(sizes, out_ref, sizes.vec_rows, a, carry[a])

    def back(count, carry):
        x = nx - 1 - count
        return tuple(backward(x, [swept_ref[x, a] for a in span], carry))

    carry = lax.fori_loop(0, nx, back, zeroed)
    for a in span:
        scatter(sizes, out_ref, sizes.vec_rows, comps + a, carry[a])


def chain_kernel(sizes, maps_ref, vec_ref, out_ref):
    comps, rows, square = sizes.comps, sizes.rows, sizes.square
    span = range(comps)

    def item(ref, chunk, part, index):
        return ref[pl.ds(part * chunk + index * rows, rows), :]

    def matrix(part, base, vector):
        return [
            combine(
                item(maps_ref, sizes.map_rows, part, base + a * comps + b) * vector[b]
                for b in span
            )
            for a in span
        ]

    carry = [jnp.zeros((rows, LANES), jnp.float32)] * comps
    incoming = []
    for part in range(sizes.parts):
        incoming.append(carry)
        for a in span:
            out_ref[pl.ds(part * sizes.vec_rows + a * rows, rows), :] = carry[a]
        moved = matrix(part, 0, carry)
        carry = [moved[a] + item(vec_ref, sizes.vec_rows, part, a) for a in span]
    carry = [jnp.zeros((rows, LANES), jnp.float32)] * comps
    for part in reversed(range(sizes.parts)):
        for a in span:
            out_ref[pl.ds(part * sizes.vec_rows + (comps + a) * rows, rows), :] = carry[a]
        moved = matrix(part, square, carry)
        mixed = matrix(part, 2 * square, incoming[part])
        carry = [
            moved[a] + (mixed[a] * GROW + item(vec_ref, sizes.vec_rows, part, comps + a))
            for a in span
        ]


def finish_kernel(sizes, residual_ref, diag_ref, lower_ref, upper_ref, vec_ref, update_ref, swept_ref):
    comps, nx = sizes.comps, sizes.nx
    span = range(comps)
    forward, backward = sweep_steps(sizes, diag_ref, lower_ref, upper_ref)
    carry = tuple(gather(sizes, vec_ref, sizes.vec_rows, a) for a in span)

    def ahead(x, carry):
        carry = forward(x, [residual_ref[x, a] for a in span], carry)
        for a in span:
            swept_ref[x, a] = carry[a]
        return tuple(carry)

    lax.fori_loop(0, nx, ahead, carry)
    carry = tuple(gather(sizes, vec_ref, sizes.vec_rows, comps + a) for a in span)

    def back(count, carry):
        x = nx - 1 - count
        carry = backward(x, [swept_ref[x, a] for a in span], carry)
        for a in span:
            update_ref[x, a] = carry[a]
        return tuple(carry)

    lax.fori_loop(0, nx, back, carry)


VMEM = pl.BlockSpec(memory_space=pltpu.VMEM)
SMEM = pl.BlockSpec(memory_space=pltpu.SMEM)


def call(kernel, name, in_specs, outs, scratch, limit, flops):
    return pl.pallas_call(
        kernel,
        name=name,
        in_specs=in_specs,
        out_specs=tuple(VMEM for _ in outs),
        out_shape=tuple(jax.ShapeDtypeStruct(shape, jnp.float32) for shape in outs),
        scratch_shapes=[pltpu.VMEM(shape, jnp.float32) for shape in scratch],
        compiler_params=pltpu.CompilerParams(vmem_limit_bytes=limit * MIB),
        cost_estimate=pl.CostEstimate(flops=flops, bytes_accessed=1 << 20, transcendentals=0),
    )


def shifted(low, high, axis, count):
    if count == 2:
        other = lax.ppermute(low, axis, [(0, 1), (1, 0)])
        return other, other
    up = [(i, i + 1) for i in range(count - 1)]
    down = [(target, origin) for origin, target in up]
    return lax.ppermute(high, axis, up), lax.ppermute(low, axis, down)


def spread(sizes, array, chunk):
    blocks = array.reshape(sizes.parts, chunk, LANES)
    moved = lax.all_to_all(blocks, "gx", split_axis=0, concat_axis=0, tiled=True)
    return moved.reshape(array.shape)


def on_device(
    state_field, source, fluid_mask, cell_kind, boundary_side_number,
    center_matrix, flux_jacobian_blocks, wall_matrix,
    diag_inverse, lower_coupling, upper_neighbour_block,
):
    sizes = Sizes(state_field.shape)
    nx, comps, ny, nz = state_field.shape
    parts = sizes.parts
    gy, gz = lax.axis_size("gy"), lax.axis_size("gz")
    gy_two, gz_two = gy == 2, gz == 2
    square = (nx, comps, comps, ny, nz)
    face = (comps, ny, nz)
    cells = nx * ny * nz

    (maps,) = call(
        functools.partial(maps_kernel, sizes), "maps", [VMEM, SMEM, SMEM],
        [(parts * sizes.map_rows, LANES)],
        [square, (2,) + square[1:], (2,) + square[1:]],
        12, 1150 * cells,
    )(diag_inverse, lower_coupling, upper_neighbour_block)

    y_count, z_count = (1 if gy_two else 2), (1 if gz_two else 2)
    masked, west, east, *rest = call(
        functools.partial(edges_kernel, sizes, gy_two, gz_two), "edges", [VMEM, VMEM],
        [state_field.shape, face, face]
        + [(nx * comps, nz)] * y_count + [(sizes.edge_rows, LANES)] * z_count,
        [], 8, 10 * cells,
    )(state_field, fluid_mask)
    y_low, y_high = rest[0], rest[y_count - 1]
    z_low, z_high = rest[y_count], rest[y_count + z_count - 1]

    from_west, from_east = shifted(west, east, "gx", parts)
    from_south, from_north = shifted(y_low, y_high, "gy", gy)
    from_below, from_above = shifted(z_low, z_high, "gz", gz)
    maps = spread(sizes, maps, sizes.map_rows)

    residual, vectors = call(
        functools.partial(residual_kernel, sizes, gy_two, gz_two), "residual",
        [VMEM] * 6 + [SMEM] * 3 + [VMEM] + [SMEM] * 2 + [VMEM] * 6,
        [state_field.shape, (parts * sizes.vec_rows, LANES)],
        [state_field.shape, (sizes.edge_rows, LANES), (sizes.edge_rows, LANES)],
        16, 650 * cells,
    )(
        state_field, masked, source, fluid_mask, cell_kind, boundary_side_number,
        center_matrix, flux_jacobian_blocks, wall_matrix,
        diag_inverse, lower_coupling, upper_neighbour_block,
        from_west, from_east, from_south, from_north, from_below, from_above,
    )
    vectors = spread(sizes, vectors, sizes.vec_rows)
    (incoming,) = call(
        functools.partial(chain_kernel, sizes), "chain", [VMEM, VMEM],
        [(parts * sizes.vec_rows, LANES)], [], 4, 1200 * ny * nz,
    )(maps, vectors)
    incoming = spread(sizes, incoming, sizes.vec_rows)
    (update,) = call(
        functools.partial(finish_kernel, sizes), "finish", [VMEM, VMEM, SMEM, SMEM, VMEM],
        [state_field.shape], [state_field.shape], 8, 200 * cells,
    )(residual, diag_inverse, lower_coupling, upper_neighbour_block, incoming)
    return update, residual


def solution(mesh):
    cells = P("gx", None, "gy", "gz")
    flags = P("gx", "gy", "gz")
    in_specs = (
        cells, cells, flags, flags, flags, P(), P(), P(),
        P("gx", None, None, "gy", "gz"), P(), P(),
    )
    return jax.shard_map(
        on_device, mesh=mesh, in_specs=in_specs, out_specs=(cells, cells), check_vma=False
    )
```

```python
import functools

import jax
import jax.numpy as jnp
from jax import lax
from jax.experimental import pallas as pl
from jax.experimental.pallas import tpu as pltpu
from jax.sharding import PartitionSpec as P

SUB = 8
LANES = 128
MIB = 1 << 20
SHRINK = 2.0**-24
GROW = 2.0**24


def round_up(value, unit):
    return -(-value // unit) * unit


class Sizes:
    def __init__(self, state_shape):
        self.nx, self.comps, self.ny, self.nz = state_shape
        self.parts = lax.axis_size("gx")
        self.vregs = self.ny // SUB
        self.rows = self.ny // self.parts
        assert self.nz == LANES and self.parts % SUB == 0
        assert self.ny % self.parts == 0
        self.square = self.comps * self.comps
        self.map_rows = round_up((3 * self.square + 2 * self.comps) * self.rows, SUB)
        self.vec_rows = round_up(2 * self.comps * self.rows, SUB)
        self.edge_count = self.nx * self.comps * self.vregs
        self.edge_rows = SUB * -(-self.edge_count // LANES)

    def start(self, index, vreg, chunk):
        first = vreg * SUB
        return (first % self.parts) * chunk + index * self.rows + first // self.parts


def scatter(sizes, ref, chunk, index, value):
    for vreg in range(sizes.vregs):
        start = sizes.start(index, vreg, chunk)
        ref[pl.ds(start, SUB, stride=chunk), :] = value[vreg * SUB : (vreg + 1) * SUB]


def gather(sizes, ref, chunk, index):
    parts = []
    for vreg in range(sizes.vregs):
        start = sizes.start(index, vreg, chunk)
        parts.append(ref[pl.ds(start, SUB, stride=chunk), :])
    return jnp.concatenate(parts, axis=0)


MOVED = ("state", "source", "mask", "kind", "side", "center", "flux", "wall", "lower", "upper")


def combine(terms):
    terms = list(terms)
    while len(terms) > 1:
        terms = [
            terms[i] + terms[i + 1] if i + 1 < len(terms) else terms[i]
            for i in range(0, len(terms), 2)
        ]
    return terms[0]


def maps_kernel(
    sizes, diag_hbm, *refs,
):
    count = len(MOVED)
    sources, out_ref, diag_ref = refs[:count], refs[count], refs[count + 1]
    targets = refs[count + 2 : 2 * count + 2]
    fwd_ref, back_ref, mix_ref, lower_ref, upper_ref, plane_sems, sems, scalar_sems = refs[2 * count + 2 :]
    comps, nx = sizes.comps, sizes.nx
    span = range(comps)
    scalars = [
        pltpu.make_async_copy(sources[MOVED.index(name)], ref, scalar_sems.at[i])
        for i, (name, ref) in enumerate((("lower", lower_ref), ("upper", upper_ref)))
    ]
    for copy in scalars:
        copy.start()

    def plane_copy(x):
        return pltpu.make_async_copy(diag_hbm.at[x], diag_ref.at[x], plane_sems.at[x])

    for x in range(nx):
        plane_copy(x).start()
    moves = [
        pltpu.make_async_copy(source, target, sems.at[i])
        for i, (source, target) in enumerate(zip(sources, targets))
    ]
    for copy in moves:
        copy.start()
    for copy in scalars:
        copy.wait()

    def product(x, coupling_ref, negate):
        sign = -1.0 if negate else 1.0
        scale = [[sign * coupling_ref[b, c] for c in span] for b in span]
        rows = []
        for a in span:
            diag = [diag_ref[x, a, b] for b in span]
            rows.append([combine(diag[b] * scale[b][c] for b in span) for c in span])
        return rows

    plane_copy(0).wait()
    first = product(0, lower_ref, False)
    for a in span:
        for c in span:
            fwd_ref[0, a, c] = first[a][c] * SHRINK

    def forward(x, carry):
        plane_copy(x).wait()
        step = product(x, lower_ref, False)
        for d in span:
            column = [fwd_ref[x - 1, c, d] for c in span]
            for a in span:
                fwd_ref[x, a, d] = combine(step[a][c] * column[c] for c in span)
        return carry

    lax.fori_loop(1, nx, forward, 0)

    last = product(nx - 1, upper_ref, True)
    for a in span:
        for d in span:
            back_ref[(nx - 1) % 2, a, d] = last[a][d]
            mix_ref[(nx - 1) % 2, a, d] = fwd_ref[nx - 1, a, d]

    def backward(count, carry):
        x = nx - 1 - count
        now, before = lax.rem(x, 2), lax.rem(x + 1, 2)
        step = product(x, upper_ref, True)
        for d in span:
            column = [back_ref[before, c, d] for c in span]
            for a in span:
                back_ref[now, a, d] = combine(step[a][c] * column[c] for c in span)
        for d in span:
            column = [mix_ref[before, c, d] for c in span]
            for a in span:
                mix_ref[now, a, d] = fwd_ref[x, a, d] + combine(
                    step[a][c] * column[c] for c in span
                )
        return carry

    lax.fori_loop(1, nx, backward, 0)

    for a in span:
        for d in span:
            index = a * comps + d
            scatter(sizes, out_ref, sizes.map_rows, index, fwd_ref[nx - 1, a, d] * GROW)
            scatter(sizes, out_ref, sizes.map_rows, sizes.square + index, back_ref[0, a, d])
            scatter(sizes, out_ref, sizes.map_rows, 2 * sizes.square + index, mix_ref[0, a, d])
    for copy in moves:
        copy.wait()


def edges_kernel(sizes, gy_two, gz_two, state_ref, mask_ref, *refs):
    masked_ref, west_ref, east_ref, *rest = refs
    y_refs = rest[: 1 if gy_two else 2]
    z_refs = rest[len(y_refs) :]
    nx, comps = sizes.nx, sizes.comps
    lane = lax.broadcasted_iota(jnp.int32, (SUB, LANES), 1)
    low_z = (lax.axis_index("gz") == 0).astype(jnp.int32)
    shifts = [low_z] if gz_two else [0, 1]
    packed = [[jnp.zeros((SUB, LANES), jnp.float32)] * (sizes.edge_rows // SUB) for _ in shifts]
    low_y = lax.axis_index("gy") == 0
    for x in range(nx):
        fluid = mask_ref[x].astype(jnp.float32)
        for c in range(comps):
            value = state_ref[x, c] * fluid
            masked_ref[x, c] = value
            if x == 0:
                west_ref[c] = value
            if x == nx - 1:
                east_ref[c] = value
            row = pl.ds(x * comps + c, 1)
            bottom, top = value[0:1], value[sizes.ny - 1 : sizes.ny]
            if gy_two:
                y_refs[0][row, :] = jnp.where(low_y, top, bottom)
            else:
                y_refs[0][row, :] = bottom
                y_refs[1][row, :] = top
            for v in range(sizes.vregs):
                index = (x * comps + c) * sizes.vregs + v
                group, place = divmod(index, LANES)
                part = value[v * SUB : (v + 1) * SUB]
                for side, shift in enumerate(shifts):
                    turned = pltpu.roll(part, lax.rem(jnp.int32(place) + shift, LANES), 1)
                    packed[side][group] = jnp.where(lane == place, turned, packed[side][group])
    for side in range(len(shifts)):
        for group, value in enumerate(packed[side]):
            z_refs[side][group * SUB : (group + 1) * SUB, :] = value


def sweep_steps(sizes, diag_ref, lower_ref, upper_ref):
    span = range(sizes.comps)

    def apply(x, vector):
        return [combine(diag_ref[x, a, b] * vector[b] for b in span) for a in span]

    def coupled(matrix_ref, vector):
        return [combine(matrix_ref[a, b] * vector[b] for b in span) for a in span]

    def forward(x, term, carry):
        pushed = coupled(lower_ref, carry)
        return apply(x, [term[a] + pushed[a] for a in span])

    def backward(x, value, carry):
        pulled = apply(x, coupled(upper_ref, carry))
        return [value[a] - pulled[a] for a in span]

    return forward, backward


def residual_kernel(
    sizes, gy_two, gz_two,
    state_ref, masked_ref, source_ref, mask_ref, kind_ref, side_ref,
    center_ref, flux_ref, wall_ref, diag_ref, lower_ref, upper_ref,
    west_ref, east_ref, south_ref, north_ref, below_ref, above_ref, maps_ref,
    residual_hbm, term_ref, out_ref, swept_ref, zlow_ref, zhigh_ref, sems,
):
    nx, comps, ny = sizes.nx, sizes.comps, sizes.ny
    span = range(comps)
    shape = (ny, LANES)
    lane = lax.broadcasted_iota(jnp.int32, (SUB, LANES), 1)
    row_index = lax.broadcasted_iota(jnp.int32, shape, 0)
    full_lane = lax.broadcasted_iota(jnp.int32, shape, 1)
    low_y = lax.axis_index("gy") == 0
    low_z = lax.axis_index("gz") == 0
    below, above = below_ref[...], above_ref[...]
    if gz_two:
        below = jnp.where(low_z, 0.0, below)
        above = jnp.where(low_z, above, 0.0)
    zlow_ref[...] = below
    zhigh_ref[...] = above
    forward, backward = sweep_steps(sizes, diag_ref, lower_ref, upper_ref)

    def edge_column(ref, x, c, target):
        parts = []
        for v in range(sizes.vregs):
            index = (x * comps + c) * sizes.vregs + v
            group = pl.multiple_of((index // LANES) * SUB, SUB)
            shift = lax.rem(target + LANES - lax.rem(index, LANES), LANES)
            parts.append(pltpu.roll(ref[pl.ds(group, SUB), :], shift, 1))
        return jnp.concatenate(parts, axis=0)

    def leave(x):
        return pltpu.make_async_copy(term_ref.at[x], residual_hbm.at[x], sems.at[x])

    def plane(x, carry):
        @pl.when(x > 0)
        def send():
            leave(x - 1).start()

        side = side_ref[x]
        fluid = mask_ref[x].astype(jnp.float32)
        kind = kind_ref[x]
        weight = fluid * jnp.where(kind == 0, 1.0, jnp.where(kind == 1, 2.0, 4.0))
        walled = side < 6
        open_face = [side != d for d in range(6)]
        total = [None] * comps

        def add(get, c, value):
            for a in span:
                term = get(a, c) * value
                total[a] = term if total[a] is None else total[a] + term

        for c in span:
            value = state_ref[x, c]
            add(lambda a, b: center_ref[a, b], c, value)
            add(lambda a, b: wall_ref[a, b], c, jnp.where(walled, value, 0.0))
            masked = masked_ref[x, c]
            row = pl.ds(x * comps + c, 1)
            south = jnp.broadcast_to(south_ref[row, :], shape)
            north = jnp.broadcast_to(north_ref[row, :], shape)
            if gy_two:
                south = jnp.where(low_y, 0.0, south)
                north = jnp.where(low_y, north, 0.0)
            neighbours = [
                jnp.where(x == 0, west_ref[c], masked_ref[jnp.maximum(x - 1, 0), c]),
                jnp.where(x == nx - 1, east_ref[c], masked_ref[jnp.minimum(x + 1, nx - 1), c]),
                jnp.where(row_index == 0, south, pltpu.roll(masked, 1, 0)),
                jnp.where(row_index == ny - 1, north, pltpu.roll(masked, ny - 1, 0)),
                jnp.where(full_lane == 0, edge_column(zlow_ref, x, c, 0), pltpu.roll(masked, 1, 1)),
                jnp.where(
                    full_lane == LANES - 1,
                    edge_column(zhigh_ref, x, c, LANES - 1),
                    pltpu.roll(masked, LANES - 1, 1),
                ),
            ]
            for d in range(6):
                add(
                    functools.partial(lambda e, a, b: flux_ref[a, e, b], d),
                    c,
                    jnp.where(open_face[d], neighbours[d], 0.0),
                )
        term = [weight * (source_ref[x, a] - total[a]) for a in span]
        for a in span:
            term_ref[x, a] = term[a]
        carry = forward(x, term, carry)
        for a in span:
            swept_ref[x, a] = carry[a]
        return tuple(carry)

    zeroed = tuple(jnp.zeros(shape, jnp.float32) for _ in span)
    carry = lax.fori_loop(0, nx, plane, zeroed)
    for a in span:
        scatter(sizes, out_ref, sizes.map_rows, 3 * sizes.square + a, carry[a])
    leave(nx - 1).start()

    def back(count, carry):
        x = nx - 1 - count
        return tuple(backward(x, [swept_ref[x, a] for a in span], carry))

    carry = lax.fori_loop(0, nx, back, zeroed)
    for a in span:
        scatter(sizes, out_ref, sizes.map_rows, 3 * sizes.square + comps + a, carry[a])
    for x in range(nx):
        leave(x).wait()


def chain_kernel(sizes, maps_ref, out_ref):
    comps, rows, square = sizes.comps, sizes.rows, sizes.square
    span = range(comps)

    def item(ref, chunk, part, index):
        return ref[pl.ds(part * chunk + index * rows, rows), :]

    def matrix(part, base, vector):
        return [
            combine(
                item(maps_ref, sizes.map_rows, part, base + a * comps + b) * vector[b]
                for b in span
            )
            for a in span
        ]

    carry = [jnp.zeros((rows, LANES), jnp.float32)] * comps
    incoming = []
    for part in range(sizes.parts):
        incoming.append(carry)
        for a in span:
            out_ref[pl.ds(part * sizes.vec_rows + a * rows, rows), :] = carry[a]
        moved = matrix(part, 0, carry)
        carry = [moved[a] + item(maps_ref, sizes.map_rows, part, 3 * square + a) for a in span]
    carry = [jnp.zeros((rows, LANES), jnp.float32)] * comps
    for part in reversed(range(sizes.parts)):
        for a in span:
            out_ref[pl.ds(part * sizes.vec_rows + (comps + a) * rows, rows), :] = carry[a]
        moved = matrix(part, square, carry)
        mixed = matrix(part, 2 * square, incoming[part])
        carry = [
            moved[a] + (mixed[a] * GROW + item(maps_ref, sizes.map_rows, part, 3 * square + comps + a))
            for a in span
        ]


def finish_kernel(
    sizes, term_ref, diag_ref, lower_ref, upper_ref, vec_ref,
    update_hbm, swept_ref, update_ref, sems,
):
    comps, nx = sizes.comps, sizes.nx
    span = range(comps)
    forward, backward = sweep_steps(sizes, diag_ref, lower_ref, upper_ref)
    carry = tuple(gather(sizes, vec_ref, sizes.vec_rows, a) for a in span)

    def leave(x):
        return pltpu.make_async_copy(update_ref.at[x], update_hbm.at[x], sems.at[x])

    def ahead(x, carry):
        carry = forward(x, [term_ref[x, a] for a in span], carry)
        for a in span:
            swept_ref[x, a] = carry[a]
        return tuple(carry)

    lax.fori_loop(0, nx, ahead, carry)
    carry = tuple(gather(sizes, vec_ref, sizes.vec_rows, comps + a) for a in span)

    def back(count, carry):
        x = nx - 1 - count

        @pl.when(count > 0)
        def send():
            leave(x + 1).start()

        carry = backward(x, [swept_ref[x, a] for a in span], carry)
        for a in span:
            update_ref[x, a] = carry[a]
        return tuple(carry)

    lax.fori_loop(0, nx, back, carry)
    leave(0).start()
    for x in range(nx):
        leave(x).wait()


VMEM = pl.BlockSpec(memory_space=pltpu.VMEM)
SMEM = pl.BlockSpec(memory_space=pltpu.SMEM)
HBM = pl.BlockSpec(memory_space=pltpu.HBM)


def floats(shape):
    return jax.ShapeDtypeStruct(shape, jnp.float32)


def call(kernel, name, in_specs, outs, scratch, limit, flops, out_specs=None, aliases=None):
    return pl.pallas_call(
        kernel,
        name=name,
        in_specs=in_specs,
        out_specs=tuple(out_specs or [VMEM] * len(outs)),
        out_shape=tuple(outs),
        scratch_shapes=scratch,
        input_output_aliases=aliases or {},
        compiler_params=pltpu.CompilerParams(vmem_limit_bytes=limit * MIB),
        cost_estimate=pl.CostEstimate(flops=flops, bytes_accessed=1 << 20, transcendentals=0),
    )


def shifted(low, high, axis, count):
    if count == 2:
        other = lax.ppermute(low, axis, [(0, 1), (1, 0)])
        return other, other
    up = [(i, i + 1) for i in range(count - 1)]
    down = [(target, origin) for origin, target in up]
    return lax.ppermute(high, axis, up), lax.ppermute(low, axis, down)


def spread(sizes, array, chunk):
    blocks = array.reshape(sizes.parts, chunk, LANES)
    moved = lax.all_to_all(blocks, "gx", split_axis=0, concat_axis=0, tiled=True)
    return moved.reshape(array.shape)


def on_device(
    state_field, source, fluid_mask, cell_kind, boundary_side_number,
    center_matrix, flux_jacobian_blocks, wall_matrix,
    diag_inverse, lower_coupling, upper_neighbour_block,
):
    sizes = Sizes(state_field.shape)
    nx, comps, ny, nz = state_field.shape
    parts = sizes.parts
    gy, gz = lax.axis_size("gy"), lax.axis_size("gz")
    gy_two, gz_two = gy == 2, gz == 2
    square = (nx, comps, comps, ny, nz)
    face = (comps, ny, nz)
    cells = nx * ny * nz
    vmem = lambda shape: pltpu.VMEM(shape, jnp.float32)

    moved = [
        state_field, source, fluid_mask, cell_kind, boundary_side_number,
        center_matrix, flux_jacobian_blocks.transpose(1, 0, 2), wall_matrix,
        lower_coupling, upper_neighbour_block,
    ]
    maps, diag, *moved = call(
        functools.partial(maps_kernel, sizes), "maps", [HBM] * (1 + len(moved)),
        [floats((parts * sizes.map_rows, LANES)), floats(square)]
        + [jax.ShapeDtypeStruct(array.shape, array.dtype) for array in moved],
        [
            vmem(square), vmem((2,) + square[1:]), vmem((2,) + square[1:]),
            pltpu.SMEM((comps, comps), jnp.float32), pltpu.SMEM((comps, comps), jnp.float32),
            pltpu.SemaphoreType.DMA((nx,)), pltpu.SemaphoreType.DMA((len(moved),)),
            pltpu.SemaphoreType.DMA((2,)),
        ],
        16, 1150 * cells,
    )(*(pltpu.with_memory_space_constraint(array, pltpu.HBM) for array in [diag_inverse] + moved))
    state, source, mask, kind, side, center, flux, wall, lower, upper = moved
    y_count, z_count = (1 if gy_two else 2), (1 if gz_two else 2)
    masked, west, east, *rest = call(
        functools.partial(edges_kernel, sizes, gy_two, gz_two), "edges", [VMEM, VMEM],
        [floats(state.shape), floats(face), floats(face)]
        + [floats((nx * comps, nz))] * y_count + [floats((sizes.edge_rows, LANES))] * z_count,
        [], 8, 10 * cells,
    )(state, mask)
    y_low, y_high = rest[0], rest[y_count - 1]
    z_low, z_high = rest[y_count], rest[y_count + z_count - 1]

    from_west, from_east = shifted(west, east, "gx", parts)
    from_south, from_north = shifted(y_low, y_high, "gy", gy)
    from_below, from_above = shifted(z_low, z_high, "gz", gz)

    residual, term, maps = call(
        functools.partial(residual_kernel, sizes, gy_two, gz_two), "residual",
        [VMEM] * 6 + [SMEM] * 3 + [VMEM] + [SMEM] * 2 + [VMEM] * 7,
        [floats(state.shape), floats(state.shape), floats(maps.shape)],
        [
            vmem(state.shape), vmem((sizes.edge_rows, LANES)), vmem((sizes.edge_rows, LANES)),
            pltpu.SemaphoreType.DMA((nx,)),
        ],
        16, 650 * cells, [HBM, VMEM, VMEM], {18: 2},
    )(
        state, masked, source, mask, kind, side, center, flux, wall, diag, lower, upper,
        from_west, from_east, from_south, from_north, from_below, from_above, maps,
    )
    maps = spread(sizes, maps, sizes.map_rows)
    (incoming,) = call(
        functools.partial(chain_kernel, sizes), "chain", [VMEM],
        [floats((parts * sizes.vec_rows, LANES))], [], 4, 1200 * ny * nz,
    )(maps)
    incoming = spread(sizes, incoming, sizes.vec_rows)
    (update,) = call(
        functools.partial(finish_kernel, sizes), "finish", [VMEM, VMEM, SMEM, SMEM, VMEM],
        [floats(state.shape)],
        [vmem(state.shape), vmem(state.shape), pltpu.SemaphoreType.DMA((nx,))],
        8, 200 * cells, [HBM],
    )(term, diag, lower, upper, incoming)
    return update, residual


def solution(mesh):
    cells = P("gx", None, "gy", "gz")
    flags = P("gx", "gy", "gz")
    in_specs = (
        cells, cells, flags, flags, flags, P(), P(), P(),
        P("gx", None, None, "gy", "gz"), P(), P(),
    )
    return jax.shard_map(
        on_device, mesh=mesh, in_specs=in_specs, out_specs=(cells, cells), check_vma=False
    )
```

```python
import functools

import jax
import jax.numpy as jnp
from jax import lax
from jax.experimental import pallas as pl
from jax.experimental.pallas import tpu as pltpu
from jax.sharding import PartitionSpec as P

SUB = 8
LANES = 128
MIB = 1 << 20
SHRINK = 2.0**-24
GROW = 2.0**24


def round_up(value, unit):
    return -(-value // unit) * unit


class Sizes:
    def __init__(self, state_shape):
        self.nx, self.comps, self.ny, self.nz = state_shape
        self.parts = lax.axis_size("gx")
        self.vregs = self.ny // SUB
        self.rows = self.ny // self.parts
        assert self.nz == LANES and self.parts % SUB == 0
        assert self.ny % self.parts == 0
        self.square = self.comps * self.comps
        self.map_rows = round_up((3 * self.square + 2 * self.comps) * self.rows, SUB)
        self.vec_rows = round_up(2 * self.comps * self.rows, SUB)
        self.edge_count = self.nx * self.comps * self.vregs
        self.edge_rows = SUB * -(-self.edge_count // LANES)

    def start(self, index, vreg, chunk):
        first = vreg * SUB
        return (first % self.parts) * chunk + index * self.rows + first // self.parts


def scatter(sizes, ref, chunk, index, value):
    for vreg in range(sizes.vregs):
        start = sizes.start(index, vreg, chunk)
        ref[pl.ds(start, SUB, stride=chunk), :] = value[vreg * SUB : (vreg + 1) * SUB]


def gather(sizes, ref, chunk, index):
    parts = []
    for vreg in range(sizes.vregs):
        start = sizes.start(index, vreg, chunk)
        parts.append(ref[pl.ds(start, SUB, stride=chunk), :])
    return jnp.concatenate(parts, axis=0)


MOVED = ("state", "source", "mask", "kind", "side")
COUPLING = ("lower", "upper")
MATRICES = ("center", "wall", "flux")


def combine(terms):
    terms = list(terms)
    while len(terms) > 1:
        terms = [
            terms[i] + terms[i + 1] if i + 1 < len(terms) else terms[i]
            for i in range(0, len(terms), 2)
        ]
    return terms[0]


def maps_kernel(sizes, diag_hbm, *refs):
    refs = list(refs)
    take = lambda count: [refs.pop(0) for _ in range(count)]
    sources = take(len(MOVED))
    lower_hbm, upper_hbm, center_hbm, wall_hbm, flux_hbm = take(5)
    out_ref, diag_ref, back_ref, mix_ref, table_ref = take(5)
    targets = take(len(MOVED) + 2)
    fwd_ref, lower_ref, upper_ref, center_ref, wall_ref, flux_ref = take(6)
    plane_sems, sems, scalar_sems = refs
    comps, nx = sizes.comps, sizes.nx
    span = range(comps)
    scalars = [
        pltpu.make_async_copy(source, target, scalar_sems.at[i])
        for i, (source, target) in enumerate(
            (
                (lower_hbm, lower_ref), (upper_hbm, upper_ref), (center_hbm, center_ref),
                (wall_hbm, wall_ref), (flux_hbm, flux_ref),
            )
        )
    ]
    for copy in scalars:
        copy.start()

    def plane_copy(x):
        return pltpu.make_async_copy(diag_hbm.at[x], diag_ref.at[x], plane_sems.at[x])

    for x in range(nx):
        plane_copy(x).start()
    moves = [
        pltpu.make_async_copy(source, target, sems.at[i])
        for i, (source, target) in enumerate(zip(sources + [lower_hbm, upper_hbm], targets))
    ]
    for copy in moves:
        copy.start()
    for copy in scalars:
        copy.wait()

    for c in span:
        for a in span:
            entries = [center_ref[a, c], wall_ref[a, c]] + [flux_ref[a, d, c] for d in range(6)]
            for d, entry in enumerate(entries):
                table_ref[d, c, a] = jnp.full((SUB, LANES), entry, jnp.float32)

    every = slice(None)
    halves = [pl.ds(v * SUB, SUB) for v in range(sizes.vregs)]

    def product(x, half, coupling_ref, negate):
        sign = -1.0 if negate else 1.0
        scale = [[sign * coupling_ref[b, c] for c in span] for b in span]
        rows = []
        for a in span:
            diag = [diag_ref[x, a, b, half] for b in span]
            rows.append([combine(diag[b] * scale[b][c] for b in span) for c in span])
        return rows

    def advance(step, source_ref, source_x, target_ref, target_x, half, added_ref=None):
        for d in span:
            column = [source_ref[source_x, c, d, half] for c in span]
            for a in span:
                value = combine(step[a][c] * column[c] for c in span)
                if added_ref is not None:
                    value = value + added_ref[target_x, a, d, half]
                target_ref[target_x, a, d, half] = value

    plane_copy(0).wait()
    for half in halves:
        first = product(0, half, lower_ref, False)
        for a in span:
            for c in span:
                fwd_ref[0, a, c, half] = first[a][c] * SHRINK

    def forward(x, carry):
        plane_copy(x).wait()
        step = product(x, every, lower_ref, False)
        advance(step, fwd_ref, x - 1, fwd_ref, x, every)
        return carry

    lax.fori_loop(1, nx, forward, 0)

    for half in halves:
        last = product(nx - 1, half, upper_ref, True)
        for a in span:
            for d in span:
                back_ref[nx - 1, a, d, half] = last[a][d]
                mix_ref[nx - 1, a, d, half] = fwd_ref[nx - 1, a, d, half]

    def backward(count, carry):
        x = nx - 1 - count
        for half in halves:
            step = product(x, half, upper_ref, True)
            advance(step, back_ref, x + 1, back_ref, x, half)
            advance(step, mix_ref, x + 1, mix_ref, x, half, fwd_ref)
        return carry

    lax.fori_loop(1, nx, backward, 0)

    for a in span:
        for d in span:
            index = a * comps + d
            scatter(sizes, out_ref, sizes.map_rows, index, fwd_ref[nx - 1, a, d] * GROW)
            scatter(sizes, out_ref, sizes.map_rows, sizes.square + index, back_ref[0, a, d])
            scatter(sizes, out_ref, sizes.map_rows, 2 * sizes.square + index, mix_ref[0, a, d])
    for copy in moves:
        copy.wait()


def edges_kernel(sizes, gy_two, gz_two, state_ref, mask_ref, *refs):
    masked_ref, west_ref, east_ref, *rest = refs
    y_refs = rest[: 1 if gy_two else 2]
    z_refs = rest[len(y_refs) :]
    nx, comps = sizes.nx, sizes.comps
    lane = lax.broadcasted_iota(jnp.int32, (SUB, LANES), 1)
    low_z = (lax.axis_index("gz") == 0).astype(jnp.int32)
    shifts = [low_z] if gz_two else [0, 1]
    packed = [[jnp.zeros((SUB, LANES), jnp.float32)] * (sizes.edge_rows // SUB) for _ in shifts]
    low_y = lax.axis_index("gy") == 0
    for x in range(nx):
        fluid = mask_ref[x].astype(jnp.float32)
        for c in range(comps):
            value = state_ref[x, c] * fluid
            masked_ref[x, c] = value
            if x == 0:
                west_ref[c] = value
            if x == nx - 1:
                east_ref[c] = value
            row = pl.ds(x * comps + c, 1)
            bottom, top = value[0:1], value[sizes.ny - 1 : sizes.ny]
            if gy_two:
                y_refs[0][row, :] = jnp.where(low_y, top, bottom)
            else:
                y_refs[0][row, :] = bottom
                y_refs[1][row, :] = top
            for v in range(sizes.vregs):
                index = (x * comps + c) * sizes.vregs + v
                group, place = divmod(index, LANES)
                part = value[v * SUB : (v + 1) * SUB]
                for side, shift in enumerate(shifts):
                    turned = pltpu.roll(part, lax.rem(jnp.int32(place) + shift, LANES), 1)
                    packed[side][group] = jnp.where(lane == place, turned, packed[side][group])
    for side in range(len(shifts)):
        for group, value in enumerate(packed[side]):
            z_refs[side][group * SUB : (group + 1) * SUB, :] = value


def sweep_steps(sizes, diag_ref, lower_ref, upper_ref):
    span = range(sizes.comps)

    def apply(x, vector):
        return [combine(diag_ref[x, a, b] * vector[b] for b in span) for a in span]

    def coupled(matrix_ref, vector):
        return [combine(matrix_ref[a, b] * vector[b] for b in span) for a in span]

    def forward(x, term, carry):
        pushed = coupled(lower_ref, carry)
        return apply(x, [term[a] + pushed[a] for a in span])

    def backward(x, value, carry):
        pulled = apply(x, coupled(upper_ref, carry))
        return [value[a] - pulled[a] for a in span]

    return forward, backward


def residual_kernel(
    sizes, gy_two, gz_two,
    state_ref, masked_ref, source_ref, mask_ref, kind_ref, side_ref,
    table_ref, diag_ref, lower_ref, upper_ref,
    west_ref, east_ref, south_ref, north_ref, below_ref, above_ref, maps_ref,
    residual_hbm, update_ref, out_ref, term_ref, swept_ref, zlow_ref, zhigh_ref, sems,
):
    nx, comps, ny = sizes.nx, sizes.comps, sizes.ny
    span = range(comps)
    shape = (ny, LANES)
    lane = lax.broadcasted_iota(jnp.int32, (SUB, LANES), 1)
    row_index = lax.broadcasted_iota(jnp.int32, shape, 0)
    full_lane = lax.broadcasted_iota(jnp.int32, shape, 1)
    low_y = lax.axis_index("gy") == 0
    low_z = lax.axis_index("gz") == 0
    below, above = below_ref[...], above_ref[...]
    if gz_two:
        below = jnp.where(low_z, 0.0, below)
        above = jnp.where(low_z, above, 0.0)
    zlow_ref[...] = below
    zhigh_ref[...] = above
    forward, backward = sweep_steps(sizes, diag_ref, lower_ref, upper_ref)

    def edge_column(ref, x, c, target):
        parts = []
        for v in range(sizes.vregs):
            index = (x * comps + c) * sizes.vregs + v
            group = pl.multiple_of((index >> 7) * SUB, SUB)
            shift = (target - index) & (LANES - 1)
            parts.append(pltpu.roll(ref[pl.ds(group, SUB), :], shift, 1))
        return jnp.concatenate(parts, axis=0)

    def leave(x):
        return pltpu.make_async_copy(term_ref.at[x], residual_hbm.at[x], sems.at[x])

    def plane(x, carry):
        @pl.when(x > 0)
        def send():
            leave(x - 1).start()

        side = side_ref[x]
        fluid = mask_ref[x].astype(jnp.float32)
        kind = kind_ref[x]
        weight = fluid * jnp.where(kind == 0, 1.0, jnp.where(kind == 1, 2.0, 4.0))
        walled = side < 6
        open_face = [side != d for d in range(6)]
        total = [None] * comps

        def add(which, c, value):
            for a in span:
                entry = table_ref[which, c, a]
                term = jnp.concatenate(
                    [entry * value[v * SUB : (v + 1) * SUB] for v in range(sizes.vregs)], axis=0
                )
                total[a] = term if total[a] is None else total[a] + term

        for c in span:
            value = state_ref[x, c]
            add(0, c, value)
            add(1, c, jnp.where(walled, value, 0.0))
            masked = masked_ref[x, c]
            row = pl.ds(x * comps + c, 1)
            south = jnp.broadcast_to(south_ref[row, :], shape)
            north = jnp.broadcast_to(north_ref[row, :], shape)
            if gy_two:
                south = jnp.where(low_y, 0.0, south)
                north = jnp.where(low_y, north, 0.0)
            neighbours = [
                jnp.where(x == 0, west_ref[c], masked_ref[jnp.maximum(x - 1, 0), c]),
                jnp.where(x == nx - 1, east_ref[c], masked_ref[jnp.minimum(x + 1, nx - 1), c]),
                jnp.where(row_index == 0, south, pltpu.roll(masked, 1, 0)),
                jnp.where(row_index == ny - 1, north, pltpu.roll(masked, ny - 1, 0)),
                jnp.where(full_lane == 0, edge_column(zlow_ref, x, c, 0), pltpu.roll(masked, 1, 1)),
                jnp.where(
                    full_lane == LANES - 1,
                    edge_column(zhigh_ref, x, c, LANES - 1),
                    pltpu.roll(masked, LANES - 1, 1),
                ),
            ]
            for d in range(6):
                add(2 + d, c, jnp.where(open_face[d], neighbours[d], 0.0))
        term = [weight * (source_ref[x, a] - total[a]) for a in span]
        for a in span:
            term_ref[x, a] = term[a]
        carry = forward(x, term, carry)
        for a in span:
            swept_ref[x, a] = carry[a]
        return tuple(carry)

    zeroed = tuple(jnp.zeros(shape, jnp.float32) for _ in span)
    carry = lax.fori_loop(0, nx, plane, zeroed)
    for a in span:
        scatter(sizes, out_ref, sizes.map_rows, 3 * sizes.square + a, carry[a])
    leave(nx - 1).start()

    def back(count, carry):
        x = nx - 1 - count
        carry = backward(x, [swept_ref[x, a] for a in span], carry)
        for a in span:
            update_ref[x, a] = carry[a]
        return tuple(carry)

    carry = lax.fori_loop(0, nx, back, zeroed)
    for a in span:
        scatter(sizes, out_ref, sizes.map_rows, 3 * sizes.square + comps + a, carry[a])
    for x in range(nx):
        leave(x).wait()


def chain_kernel(sizes, maps_ref, out_ref):
    comps, rows, square = sizes.comps, sizes.rows, sizes.square
    span = range(comps)

    def item(ref, chunk, part, index):
        return ref[pl.ds(part * chunk + index * rows, rows), :]

    def matrix(part, base, vector):
        return [
            combine(
                item(maps_ref, sizes.map_rows, part, base + a * comps + b) * vector[b]
                for b in span
            )
            for a in span
        ]

    carry = [jnp.zeros((rows, LANES), jnp.float32)] * comps
    incoming = []
    for part in range(sizes.parts):
        incoming.append(carry)
        for a in span:
            out_ref[pl.ds(part * sizes.vec_rows + a * rows, rows), :] = carry[a]
        moved = matrix(part, 0, carry)
        carry = [moved[a] + item(maps_ref, sizes.map_rows, part, 3 * square + a) for a in span]
    carry = [jnp.zeros((rows, LANES), jnp.float32)] * comps
    for part in reversed(range(sizes.parts)):
        for a in span:
            out_ref[pl.ds(part * sizes.vec_rows + (comps + a) * rows, rows), :] = carry[a]
        moved = matrix(part, square, carry)
        mixed = matrix(part, 2 * square, incoming[part])
        carry = [
            moved[a] + (mixed[a] * GROW + item(maps_ref, sizes.map_rows, part, 3 * square + comps + a))
            for a in span
        ]


def finish_kernel(sizes, base_ref, back_ref, mix_ref, vec_ref, update_hbm, update_ref, sems):
    comps, nx = sizes.comps, sizes.nx
    span = range(comps)
    ahead = [gather(sizes, vec_ref, sizes.vec_rows, a) for a in span]
    behind = [gather(sizes, vec_ref, sizes.vec_rows, comps + a) for a in span]

    def leave(x):
        return pltpu.make_async_copy(update_ref.at[x], update_hbm.at[x], sems.at[x])

    def plane(x, carry):
        @pl.when(x > 0)
        def send():
            leave(x - 1).start()

        for a in span:
            mixed = combine(mix_ref[x, a, b] * carry[b] for b in span)
            moved = combine(back_ref[x, a, b] * carry[comps + b] for b in span)
            update_ref[x, a] = base_ref[x, a] + (mixed * GROW + moved)
        return carry

    lax.fori_loop(0, nx, plane, tuple(ahead + behind))
    leave(nx - 1).start()
    for x in range(nx):
        leave(x).wait()


VMEM = pl.BlockSpec(memory_space=pltpu.VMEM)
SMEM = pl.BlockSpec(memory_space=pltpu.SMEM)
HBM = pl.BlockSpec(memory_space=pltpu.HBM)


def floats(shape):
    return jax.ShapeDtypeStruct(shape, jnp.float32)


def call(kernel, name, in_specs, outs, scratch, limit, flops, out_specs=None, aliases=None):
    return pl.pallas_call(
        kernel,
        name=name,
        in_specs=in_specs,
        out_specs=tuple(out_specs or [VMEM] * len(outs)),
        out_shape=tuple(outs),
        scratch_shapes=scratch,
        input_output_aliases=aliases or {},
        compiler_params=pltpu.CompilerParams(vmem_limit_bytes=limit * MIB),
        cost_estimate=pl.CostEstimate(flops=flops, bytes_accessed=1 << 20, transcendentals=0),
    )


def shifted(low, high, axis, count):
    if count == 2:
        other = lax.ppermute(low, axis, [(0, 1), (1, 0)])
        return other, other
    up = [(i, i + 1) for i in range(count - 1)]
    down = [(target, origin) for origin, target in up]
    return lax.ppermute(high, axis, up), lax.ppermute(low, axis, down)


def spread(sizes, array, chunk):
    blocks = array.reshape(sizes.parts, chunk, LANES)
    moved = lax.all_to_all(blocks, "gx", split_axis=0, concat_axis=0, tiled=True)
    return moved.reshape(array.shape)


def on_device(
    state_field, source, fluid_mask, cell_kind, boundary_side_number,
    center_matrix, flux_jacobian_blocks, wall_matrix,
    diag_inverse, lower_coupling, upper_neighbour_block,
):
    sizes = Sizes(state_field.shape)
    nx, comps, ny, nz = state_field.shape
    parts = sizes.parts
    gy, gz = lax.axis_size("gy"), lax.axis_size("gz")
    gy_two, gz_two = gy == 2, gz == 2
    square = (nx, comps, comps, ny, nz)
    face = (comps, ny, nz)
    cells = nx * ny * nz
    vmem = lambda shape: pltpu.VMEM(shape, jnp.float32)

    moved = [state_field, source, fluid_mask, cell_kind, boundary_side_number]
    coupling = [lower_coupling, upper_neighbour_block]
    matrices = [center_matrix, wall_matrix, flux_jacobian_blocks.transpose(1, 0, 2)]
    operands = [diag_inverse] + moved + coupling + matrices
    smem = lambda shape: pltpu.SMEM(shape, jnp.float32)
    table = (8, comps, comps, SUB, LANES)
    maps, diag, back, mix, table, *moved = call(
        functools.partial(maps_kernel, sizes), "maps", [HBM] * len(operands),
        [floats((parts * sizes.map_rows, LANES)), floats(square), floats(square), floats(square)]
        + [floats(table)]
        + [jax.ShapeDtypeStruct(array.shape, array.dtype) for array in moved + coupling],
        [vmem(square)]
        + [smem(array.shape) for array in coupling + matrices]
        + [
            pltpu.SemaphoreType.DMA((nx,)), pltpu.SemaphoreType.DMA((len(moved + coupling),)),
            pltpu.SemaphoreType.DMA((5,)),
        ],
        24, 1150 * cells,
    )(*(pltpu.with_memory_space_constraint(array, pltpu.HBM) for array in operands))
    state, source, mask, kind, side, lower, upper = moved

    y_count, z_count = (1 if gy_two else 2), (1 if gz_two else 2)
    masked, west, east, *rest = call(
        functools.partial(edges_kernel, sizes, gy_two, gz_two), "edges", [VMEM, VMEM],
        [floats(state.shape), floats(face), floats(face)]
        + [floats((nx * comps, nz))] * y_count + [floats((sizes.edge_rows, LANES))] * z_count,
        [], 8, 10 * cells,
    )(state, mask)
    y_low, y_high = rest[0], rest[y_count - 1]
    z_low, z_high = rest[y_count], rest[y_count + z_count - 1]

    from_west, from_east = shifted(west, east, "gx", parts)
    from_south, from_north = shifted(y_low, y_high, "gy", gy)
    from_below, from_above = shifted(z_low, z_high, "gz", gz)

    residual, base, maps = call(
        functools.partial(residual_kernel, sizes, gy_two, gz_two), "residual",
        [VMEM] * 8 + [SMEM] * 2 + [VMEM] * 7,
        [floats(state.shape), floats(state.shape), floats(maps.shape)],
        [
            vmem(state.shape), vmem(state.shape),
            vmem((sizes.edge_rows, LANES)), vmem((sizes.edge_rows, LANES)),
            pltpu.SemaphoreType.DMA((nx,)),
        ],
        16, 650 * cells, [HBM, VMEM, VMEM], {16: 2},
    )(
        state, masked, source, mask, kind, side, table, diag, lower, upper,
        from_west, from_east, from_south, from_north, from_below, from_above, maps,
    )
    maps = spread(sizes, maps, sizes.map_rows)
    (incoming,) = call(
        functools.partial(chain_kernel, sizes), "chain", [VMEM],
        [floats((parts * sizes.vec_rows, LANES))], [], 4, 1200 * ny * nz,
    )(maps)
    incoming = spread(sizes, incoming, sizes.vec_rows)
    (update,) = call(
        functools.partial(finish_kernel, sizes), "finish", [VMEM] * 4,
        [floats(state.shape)],
        [vmem(state.shape), pltpu.SemaphoreType.DMA((nx,))],
        16, 200 * cells, [HBM],
    )(base, back, mix, incoming)
    return update, residual


def solution(mesh):
    cells = P("gx", None, "gy", "gz")
    flags = P("gx", "gy", "gz")
    in_specs = (
        cells, cells, flags, flags, flags, P(), P(), P(),
        P("gx", None, None, "gy", "gz"), P(), P(),
    )
    return jax.shard_map(
        on_device, mesh=mesh, in_specs=in_specs, out_specs=(cells, cells), check_vma=False
    )
```

```python
import functools

import jax
import jax.numpy as jnp
from jax import lax
from jax.experimental import pallas as pl
from jax.experimental.pallas import tpu as pltpu
from jax.sharding import PartitionSpec as P

SUB = 8
LANES = 128
MIB = 1 << 20
SHRINK = 2.0**-24
GROW = 2.0**24


def round_up(value, unit):
    return -(-value // unit) * unit


class Sizes:
    def __init__(self, state_shape):
        self.nx, self.comps, self.ny, self.nz = state_shape
        self.parts = lax.axis_size("gx")
        self.vregs = self.ny // SUB
        self.rows = SUB // 2
        self.group = self.ny // self.rows
        assert self.nz == LANES and self.ny % SUB == 0 and self.parts % 2 == 0
        assert self.parts % self.group == 0
        self.square = self.comps * self.comps
        self.vectors = 2 * self.comps
        self.chunk = round_up((self.vectors + 3 * self.square) * self.rows, SUB)
        self.vec_rows = round_up(self.vectors * self.rows, SUB)
        self.hop_rows = round_up(self.comps * self.rows, SUB)
        self.edge_count = self.nx * self.comps * self.vregs
        self.edge_rows = SUB * -(-self.edge_count // LANES)


def scatter(sizes, ref, index, values):
    half = SUB // 2
    low = lax.broadcasted_iota(jnp.int32, (SUB, LANES), 0) < half
    for i in range(0, len(values), 2):
        first, second = values[i], values[min(i + 1, len(values) - 1)]
        for v in range(sizes.vregs):
            one, two = (value[v * SUB : (v + 1) * SUB] for value in (first, second))
            start = 2 * v * sizes.chunk + (index + i) * half
            ref[start : start + SUB, :] = jnp.where(low, one, pltpu.roll(two, half, 0))
            start += sizes.chunk
            ref[start : start + SUB, :] = jnp.where(low, pltpu.roll(one, half, 0), two)


def gather(sizes, ref, index):
    half = SUB // 2
    parts = []
    for part in range(sizes.group):
        start = part * sizes.vec_rows + index * half
        parts.append(ref[start : start + half, :])
    return jnp.concatenate(parts, axis=0)


MOVED = ("state", "source", "mask", "kind", "side")
COUPLING = ("lower", "upper")
MATRICES = ("center", "wall", "flux")


def combine(terms):
    terms = list(terms)
    while len(terms) > 1:
        terms = [
            terms[i] + terms[i + 1] if i + 1 < len(terms) else terms[i]
            for i in range(0, len(terms), 2)
        ]
    return terms[0]


def maps_kernel(sizes, diag_hbm, *refs):
    refs = list(refs)
    take = lambda count: [refs.pop(0) for _ in range(count)]
    sources = take(len(MOVED))
    lower_hbm, upper_hbm, center_hbm, wall_hbm, flux_hbm = take(5)
    out_ref, diag_ref, back_ref, mix_ref, table_ref = take(5)
    targets = take(len(MOVED) + 2)
    fwd_ref, lower_ref, upper_ref, center_ref, wall_ref, flux_ref = take(6)
    plane_sems, sems, scalar_sems = refs
    comps, nx = sizes.comps, sizes.nx
    span = range(comps)
    scalars = [
        pltpu.make_async_copy(source, target, scalar_sems.at[i])
        for i, (source, target) in enumerate(
            (
                (lower_hbm, lower_ref), (upper_hbm, upper_ref), (center_hbm, center_ref),
                (wall_hbm, wall_ref), (flux_hbm, flux_ref),
            )
        )
    ]
    for copy in scalars:
        copy.start()

    def plane_copy(x):
        return pltpu.make_async_copy(diag_hbm.at[x], diag_ref.at[x], plane_sems.at[x])

    for x in range(nx):
        plane_copy(x).start()
    moves = [
        pltpu.make_async_copy(source, target, sems.at[i])
        for i, (source, target) in enumerate(zip(sources + [lower_hbm, upper_hbm], targets))
    ]
    for copy in moves:
        copy.start()
    for copy in scalars:
        copy.wait()

    for c in span:
        for a in span:
            entries = [center_ref[a, c], wall_ref[a, c]] + [flux_ref[a, d, c] for d in range(6)]
            for d, entry in enumerate(entries):
                table_ref[d, c, a] = jnp.full((SUB, LANES), entry, jnp.float32)

    every = slice(None)
    halves = [pl.ds(v * SUB, SUB) for v in range(sizes.vregs)]

    def product(x, half, coupling_ref, negate):
        sign = -1.0 if negate else 1.0
        scale = [[sign * coupling_ref[b, c] for c in span] for b in span]
        rows = []
        for a in span:
            diag = [diag_ref[x, a, b, half] for b in span]
            rows.append([combine(diag[b] * scale[b][c] for b in span) for c in span])
        return rows

    def advance(step, source_ref, source_x, target_ref, target_x, half, added_ref=None):
        for d in span:
            column = [source_ref[source_x, c, d, half] for c in span]
            for a in span:
                value = combine(step[a][c] * column[c] for c in span)
                if added_ref is not None:
                    value = value + added_ref[target_x, a, d, half]
                target_ref[target_x, a, d, half] = value

    plane_copy(0).wait()
    for half in halves:
        first = product(0, half, lower_ref, False)
        for a in span:
            for c in span:
                fwd_ref[0, a, c, half] = first[a][c] * SHRINK

    def forward(x, carry):
        plane_copy(x).wait()
        step = product(x, every, lower_ref, False)
        advance(step, fwd_ref, x - 1, fwd_ref, x, every)
        return carry

    lax.fori_loop(1, nx, forward, 0)

    for half in halves:
        last = product(nx - 1, half, upper_ref, True)
        for a in span:
            for d in span:
                back_ref[nx - 1, a, d, half] = last[a][d]
                mix_ref[nx - 1, a, d, half] = fwd_ref[nx - 1, a, d, half]

    def backward(count, carry):
        x = nx - 1 - count
        for half in halves:
            step = product(x, half, upper_ref, True)
            advance(step, back_ref, x + 1, back_ref, x, half)
            advance(step, mix_ref, x + 1, mix_ref, x, half, fwd_ref)
        return carry

    lax.fori_loop(1, nx, backward, 0)

    pairs = [(a, d) for a in span for d in span]
    scatter(
        sizes, out_ref, sizes.vectors,
        [fwd_ref[nx - 1, a, d] * GROW for a, d in pairs]
        + [back_ref[0, a, d] for a, d in pairs]
        + [mix_ref[0, a, d] for a, d in pairs],
    )
    for copy in moves:
        copy.wait()


def edges_kernel(sizes, gy_two, gz_two, state_ref, mask_ref, *refs):
    masked_ref, inner_ref, outer_ref, *rest = refs
    y_refs = rest[: 1 if gy_two else 2]
    z_refs = rest[len(y_refs) :]
    nx, comps = sizes.nx, sizes.comps
    lane = lax.broadcasted_iota(jnp.int32, (SUB, LANES), 1)
    low_z = (lax.axis_index("gz") == 0).astype(jnp.int32)
    shifts = [low_z] if gz_two else [0, 1]
    packed = [[jnp.zeros((SUB, LANES), jnp.float32)] * (sizes.edge_rows // SUB) for _ in shifts]
    low_y = lax.axis_index("gy") == 0
    even = lax.rem(lax.axis_index("gx"), 2) == 0
    first = []
    for x in range(nx):
        fluid = mask_ref[x].astype(jnp.float32)
        for c in range(comps):
            value = state_ref[x, c] * fluid
            masked_ref[x, c] = value
            if x == 0:
                first.append(value)
            if x == nx - 1:
                inner_ref[c] = jnp.where(even, value, first[c])
                outer_ref[c] = jnp.where(even, first[c], value)
            row = pl.ds(x * comps + c, 1)
            bottom, top = value[0:1], value[sizes.ny - 1 : sizes.ny]
            if gy_two:
                y_refs[0][row, :] = jnp.where(low_y, top, bottom)
            else:
                y_refs[0][row, :] = bottom
                y_refs[1][row, :] = top
            for v in range(sizes.vregs):
                index = (x * comps + c) * sizes.vregs + v
                group, place = divmod(index, LANES)
                part = value[v * SUB : (v + 1) * SUB]
                for side, shift in enumerate(shifts):
                    turned = pltpu.roll(part, lax.rem(jnp.int32(place) + shift, LANES), 1)
                    packed[side][group] = jnp.where(lane == place, turned, packed[side][group])
    for side in range(len(shifts)):
        for group, value in enumerate(packed[side]):
            z_refs[side][group * SUB : (group + 1) * SUB, :] = value


def sweep_steps(sizes, diag_ref, lower_ref, upper_ref):
    span = range(sizes.comps)

    def apply(x, vector):
        return [combine(diag_ref[x, a, b] * vector[b] for b in span) for a in span]

    def coupled(matrix_ref, vector):
        return [combine(matrix_ref[a, b] * vector[b] for b in span) for a in span]

    def forward(x, term, carry):
        pushed = coupled(lower_ref, carry)
        return apply(x, [term[a] + pushed[a] for a in span])

    def backward(x, value, carry):
        pulled = apply(x, coupled(upper_ref, carry))
        return [value[a] - pulled[a] for a in span]

    return forward, backward


def residual_kernel(
    sizes, gy_two, gz_two,
    state_ref, masked_ref, source_ref, mask_ref, kind_ref, side_ref,
    table_ref, diag_ref, lower_ref, upper_ref,
    inner_ref, outer_ref, south_ref, north_ref, below_ref, above_ref, maps_ref,
    residual_hbm, update_ref, out_ref,
    term_ref, swept_ref, zlow_ref, zhigh_ref, west_ref, east_ref, sems,
):
    nx, comps, ny = sizes.nx, sizes.comps, sizes.ny
    span = range(comps)
    shape = (ny, LANES)
    lane = lax.broadcasted_iota(jnp.int32, (SUB, LANES), 1)
    row_index = lax.broadcasted_iota(jnp.int32, shape, 0)
    full_lane = lax.broadcasted_iota(jnp.int32, shape, 1)
    low_y = lax.axis_index("gy") == 0
    low_z = lax.axis_index("gz") == 0
    below, above = below_ref[...], above_ref[...]
    if gz_two:
        below = jnp.where(low_z, 0.0, below)
        above = jnp.where(low_z, above, 0.0)
    zlow_ref[...] = below
    zhigh_ref[...] = above
    even = lax.rem(lax.axis_index("gx"), 2) == 0
    for c in span:
        inner, outer = inner_ref[c], outer_ref[c]
        west_ref[c] = jnp.where(even, outer, inner)
        east_ref[c] = jnp.where(even, inner, outer)
    forward, backward = sweep_steps(sizes, diag_ref, lower_ref, upper_ref)

    def edge_column(ref, x, c, target):
        parts = []
        for v in range(sizes.vregs):
            index = (x * comps + c) * sizes.vregs + v
            group = pl.multiple_of((index >> 7) * SUB, SUB)
            shift = (target - index) & (LANES - 1)
            parts.append(pltpu.roll(ref[pl.ds(group, SUB), :], shift, 1))
        return jnp.concatenate(parts, axis=0)

    def leave(x):
        return pltpu.make_async_copy(term_ref.at[x], residual_hbm.at[x], sems.at[x])

    def plane(x, carry):
        @pl.when(x > 0)
        def send():
            leave(x - 1).start()

        side = side_ref[x]
        fluid = mask_ref[x].astype(jnp.float32)
        kind = kind_ref[x]
        weight = fluid * jnp.where(kind == 0, 1.0, jnp.where(kind == 1, 2.0, 4.0))
        walled = side < 6
        open_face = [side != d for d in range(6)]
        total = [None] * comps

        def add(which, c, value):
            for a in span:
                entry = table_ref[which, c, a]
                term = jnp.concatenate(
                    [entry * value[v * SUB : (v + 1) * SUB] for v in range(sizes.vregs)], axis=0
                )
                total[a] = term if total[a] is None else total[a] + term

        for c in span:
            value = state_ref[x, c]
            add(0, c, value)
            add(1, c, jnp.where(walled, value, 0.0))
            masked = masked_ref[x, c]
            row = pl.ds(x * comps + c, 1)
            south = jnp.broadcast_to(south_ref[row, :], shape)
            north = jnp.broadcast_to(north_ref[row, :], shape)
            if gy_two:
                south = jnp.where(low_y, 0.0, south)
                north = jnp.where(low_y, north, 0.0)
            neighbours = [
                jnp.where(x == 0, west_ref[c], masked_ref[jnp.maximum(x - 1, 0), c]),
                jnp.where(x == nx - 1, east_ref[c], masked_ref[jnp.minimum(x + 1, nx - 1), c]),
                jnp.where(row_index == 0, south, pltpu.roll(masked, 1, 0)),
                jnp.where(row_index == ny - 1, north, pltpu.roll(masked, ny - 1, 0)),
                jnp.where(full_lane == 0, edge_column(zlow_ref, x, c, 0), pltpu.roll(masked, 1, 1)),
                jnp.where(
                    full_lane == LANES - 1,
                    edge_column(zhigh_ref, x, c, LANES - 1),
                    pltpu.roll(masked, LANES - 1, 1),
                ),
            ]
            for d in range(6):
                add(2 + d, c, jnp.where(open_face[d], neighbours[d], 0.0))
        term = [weight * (source_ref[x, a] - total[a]) for a in span]
        for a in span:
            term_ref[x, a] = term[a]
        carry = forward(x, term, carry)
        for a in span:
            swept_ref[x, a] = carry[a]
        return tuple(carry)

    zeroed = tuple(jnp.zeros(shape, jnp.float32) for _ in span)
    ahead = lax.fori_loop(0, nx, plane, zeroed)
    leave(nx - 1).start()

    def back(count, carry):
        x = nx - 1 - count
        carry = backward(x, [swept_ref[x, a] for a in span], carry)
        for a in span:
            update_ref[x, a] = carry[a]
        return tuple(carry)

    behind = lax.fori_loop(0, nx, back, zeroed)
    scatter(sizes, out_ref, 0, list(ahead) + list(behind))
    for x in range(nx):
        leave(x).wait()


def chain(sizes, maps_ref):
    comps, rows, square = sizes.comps, sizes.rows, sizes.square
    span = range(comps)

    def item(part, index):
        start = part * sizes.chunk + index * rows
        return maps_ref[start : start + rows, :]

    def matrix(part, which, vector):
        base = sizes.vectors + which * square
        return [combine(item(part, base + a * comps + b) * vector[b] for b in span) for a in span]

    def ahead(carry):
        entering = []
        for part in range(sizes.group):
            entering.append(carry)
            moved = matrix(part, 0, carry)
            carry = [moved[a] + item(part, a) for a in span]
        return entering, carry

    def behind(carry, ahead_entering):
        entering = []
        for part in reversed(range(sizes.group)):
            entering.insert(0, carry)
            moved = matrix(part, 1, carry)
            mixed = matrix(part, 2, ahead_entering[part])
            carry = [moved[a] + (mixed[a] * GROW + item(part, comps + a)) for a in span]
        return entering, carry

    return ahead, behind


def hop_values(sizes, ref):
    rows = sizes.rows
    return [ref[a * rows : (a + 1) * rows, :] for a in range(sizes.comps)]


def hop_store(sizes, ref, values):
    for a, value in enumerate(values):
        ref[a * sizes.rows : (a + 1) * sizes.rows, :] = value


def ahead_kernel(sizes, entered, maps_ref, *refs):
    *in_refs, out_ref = refs
    zero = [jnp.zeros((sizes.rows, LANES), jnp.float32)] * sizes.comps
    ahead, behind = chain(sizes, maps_ref)
    hop_store(sizes, out_ref, ahead(hop_values(sizes, in_refs[0]) if entered else zero)[1])


def behind_kernel(sizes, entered, last, maps_ref, ahead_ref, *refs):
    *in_refs, out_ref = refs
    zero = [jnp.zeros((sizes.rows, LANES), jnp.float32)] * sizes.comps
    ahead, behind = chain(sizes, maps_ref)
    forward, unused = ahead(hop_values(sizes, ahead_ref) if ahead_ref is not None else zero)
    backward, leaving = behind(hop_values(sizes, in_refs[0]) if entered else zero, forward)
    if not last:
        hop_store(sizes, out_ref, leaving)
        return
    rows = sizes.rows
    for part in range(sizes.group):
        for i, value in enumerate(forward[part] + backward[part]):
            start = part * sizes.vec_rows + i * rows
            out_ref[start : start + rows, :] = value


def finish_kernel(sizes, base_ref, back_ref, mix_ref, vec_ref, update_hbm, update_ref, sems):
    comps, nx = sizes.comps, sizes.nx
    span = range(comps)
    ahead = [gather(sizes, vec_ref, a) for a in span]
    behind = [gather(sizes, vec_ref, comps + a) for a in span]

    def leave(x):
        return pltpu.make_async_copy(update_ref.at[x], update_hbm.at[x], sems.at[x])

    def plane(x, carry):
        @pl.when(x > 0)
        def send():
            leave(x - 1).start()

        for a in span:
            mixed = combine(mix_ref[x, a, b] * carry[b] for b in span)
            moved = combine(back_ref[x, a, b] * carry[comps + b] for b in span)
            update_ref[x, a] = base_ref[x, a] + (mixed * GROW + moved)
        return carry

    lax.fori_loop(0, nx, plane, tuple(ahead + behind))
    leave(nx - 1).start()
    for x in range(nx):
        leave(x).wait()


VMEM = pl.BlockSpec(memory_space=pltpu.VMEM)
SMEM = pl.BlockSpec(memory_space=pltpu.SMEM)
HBM = pl.BlockSpec(memory_space=pltpu.HBM)


def floats(shape):
    return jax.ShapeDtypeStruct(shape, jnp.float32)


def call(kernel, name, in_specs, outs, scratch, limit, flops, out_specs=None, aliases=None):
    return pl.pallas_call(
        kernel,
        name=name,
        in_specs=in_specs,
        out_specs=tuple(out_specs or [VMEM] * len(outs)),
        out_shape=tuple(outs),
        scratch_shapes=scratch,
        input_output_aliases=aliases or {},
        compiler_params=pltpu.CompilerParams(vmem_limit_bytes=limit * MIB),
        cost_estimate=pl.CostEstimate(flops=flops, bytes_accessed=1 << 20, transcendentals=0),
    )


def shifted(low, high, axis, count):
    if count == 2:
        other = lax.ppermute(low, axis, [(0, 1), (1, 0)])
        return other, other
    up = [(i, i + 1) for i in range(count - 1)]
    down = [(target, origin) for origin, target in up]
    return lax.ppermute(high, axis, up), lax.ppermute(low, axis, down)


def swapped(inner, outer, count):
    pairs = lambda first: [(i, i + 1) for i in range(first, count - 1, 2)]
    both = lambda first: pairs(first) + [(target, origin) for origin, target in pairs(first)]
    return lax.ppermute(inner, "gx", both(0)), lax.ppermute(outer, "gx", both(1))


def spread(sizes, array, chunk):
    blocks = array.reshape(sizes.group, chunk, LANES)
    groups = [
        list(range(first, first + sizes.group)) for first in range(0, sizes.parts, sizes.group)
    ]
    moved = lax.all_to_all(
        blocks, "gx", split_axis=0, concat_axis=0, tiled=True, axis_index_groups=groups
    )
    return moved.reshape(array.shape)


def solve_chain(sizes, maps):
    hop = floats((sizes.hop_rows, LANES))
    up = [(i, i + sizes.group) for i in range(sizes.parts - sizes.group)]
    down = [(target, origin) for origin, target in up]
    flops = 300 * sizes.group * sizes.rows * LANES
    steps = sizes.parts // sizes.group - 1
    ahead = []
    for step in range(steps):
        (leaving,) = call(
            functools.partial(ahead_kernel, sizes, bool(ahead)), "ahead",
            [VMEM] * (1 + len(ahead)), [hop], [], 4, flops,
        )(maps, *ahead)
        ahead = [lax.ppermute(leaving, "gx", up)]
    behind = []
    for step in range(steps + 1):
        last = step == steps
        kernel = functools.partial(behind_kernel, sizes, bool(behind), last)
        if not ahead:
            kernel = functools.partial(
                lambda inner, maps_ref, *refs: inner(maps_ref, None, *refs), kernel
            )
        out = floats((sizes.group * sizes.vec_rows, LANES)) if last else hop
        (leaving,) = call(
            kernel, "behind", [VMEM] * (1 + len(ahead) + len(behind)), [out], [], 4, flops
        )(maps, *ahead, *behind)
        if not last:
            behind = [lax.ppermute(leaving, "gx", down)]
    return leaving


def on_device(
    state_field, source, fluid_mask, cell_kind, boundary_side_number,
    center_matrix, flux_jacobian_blocks, wall_matrix,
    diag_inverse, lower_coupling, upper_neighbour_block,
):
    sizes = Sizes(state_field.shape)
    nx, comps, ny, nz = state_field.shape
    parts = sizes.parts
    gy, gz = lax.axis_size("gy"), lax.axis_size("gz")
    gy_two, gz_two = gy == 2, gz == 2
    square = (nx, comps, comps, ny, nz)
    face = (comps, ny, nz)
    cells = nx * ny * nz
    vmem = lambda shape: pltpu.VMEM(shape, jnp.float32)

    moved = [state_field, source, fluid_mask, cell_kind, boundary_side_number]
    coupling = [lower_coupling, upper_neighbour_block]
    matrices = [center_matrix, wall_matrix, flux_jacobian_blocks.transpose(1, 0, 2)]
    operands = [diag_inverse] + moved + coupling + matrices
    smem = lambda shape: pltpu.SMEM(shape, jnp.float32)
    table = (8, comps, comps, SUB, LANES)
    maps, diag, back, mix, table, *moved = call(
        functools.partial(maps_kernel, sizes), "maps", [HBM] * len(operands),
        [floats((sizes.group * sizes.chunk, LANES)), floats(square), floats(square), floats(square)]
        + [floats(table)]
        + [jax.ShapeDtypeStruct(array.shape, array.dtype) for array in moved + coupling],
        [vmem(square)]
        + [smem(array.shape) for array in coupling + matrices]
        + [
            pltpu.SemaphoreType.DMA((nx,)), pltpu.SemaphoreType.DMA((len(moved + coupling),)),
            pltpu.SemaphoreType.DMA((5,)),
        ],
        24, 1150 * cells,
    )(*(pltpu.with_memory_space_constraint(array, pltpu.HBM) for array in operands))
    state, source, mask, kind, side, lower, upper = moved

    y_count, z_count = (1 if gy_two else 2), (1 if gz_two else 2)
    masked, inner, outer, *rest = call(
        functools.partial(edges_kernel, sizes, gy_two, gz_two), "edges", [VMEM, VMEM],
        [floats(state.shape), floats(face), floats(face)]
        + [floats((nx * comps, nz))] * y_count + [floats((sizes.edge_rows, LANES))] * z_count,
        [], 8, 10 * cells,
    )(state, mask)
    y_low, y_high = rest[0], rest[y_count - 1]
    z_low, z_high = rest[y_count], rest[y_count + z_count - 1]

    from_inner, from_outer = swapped(inner, outer, parts)
    from_south, from_north = shifted(y_low, y_high, "gy", gy)
    from_below, from_above = shifted(z_low, z_high, "gz", gz)

    residual, base, maps = call(
        functools.partial(residual_kernel, sizes, gy_two, gz_two), "residual",
        [VMEM] * 8 + [SMEM] * 2 + [VMEM] * 7,
        [floats(state.shape), floats(state.shape), floats(maps.shape)],
        [
            vmem(state.shape), vmem(state.shape),
            vmem((sizes.edge_rows, LANES)), vmem((sizes.edge_rows, LANES)),
            vmem(face), vmem(face),
            pltpu.SemaphoreType.DMA((nx,)),
        ],
        16, 650 * cells, [HBM, VMEM, VMEM], {16: 2},
    )(
        state, masked, source, mask, kind, side, table, diag, lower, upper,
        from_inner, from_outer, from_south, from_north, from_below, from_above, maps,
    )
    maps = spread(sizes, maps, sizes.chunk)
    incoming = spread(sizes, solve_chain(sizes, maps), sizes.vec_rows)
    (update,) = call(
        functools.partial(finish_kernel, sizes), "finish", [VMEM] * 4,
        [floats(state.shape)],
        [vmem(state.shape), pltpu.SemaphoreType.DMA((nx,))],
        16, 200 * cells, [HBM],
    )(base, back, mix, incoming)
    return update, residual


def solution(mesh):
    cells = P("gx", None, "gy", "gz")
    flags = P("gx", "gy", "gz")
    in_specs = (
        cells, cells, flags, flags, flags, P(), P(), P(),
        P("gx", None, None, "gy", "gz"), P(), P(),
    )
    return jax.shard_map(
        on_device, mesh=mesh, in_specs=in_specs, out_specs=(cells, cells), check_vma=False
    )
```

```python
import functools

import jax
import jax.numpy as jnp
from jax import lax
from jax.experimental import pallas as pl
from jax.experimental.pallas import tpu as pltpu
from jax.sharding import PartitionSpec as P

SUB = 8
LANES = 128
MIB = 1 << 20
SHRINK = 2.0**-24
GROW = 2.0**24


def round_up(value, unit):
    return -(-value // unit) * unit


class Sizes:
    def __init__(self, state_shape):
        self.nx, self.comps, self.ny, self.nz = state_shape
        self.parts = lax.axis_size("gx")
        self.vregs = self.ny // SUB
        self.rows = SUB // 2
        self.group = self.ny // self.rows
        assert self.nz == LANES and self.ny % SUB == 0 and self.parts % 2 == 0
        assert self.parts % self.group == 0
        self.square = self.comps * self.comps
        self.vectors = 2 * self.comps
        self.chunk = round_up((self.vectors + 3 * self.square) * self.rows, SUB)
        self.vec_rows = round_up(self.vectors * self.rows, SUB)
        self.hop_rows = round_up(self.comps * self.rows, SUB)
        self.edge_count = self.nx * self.comps * self.vregs
        self.edge_rows = SUB * -(-self.edge_count // LANES)


def scatter(sizes, ref, index, values):
    half = SUB // 2
    low = lax.broadcasted_iota(jnp.int32, (SUB, LANES), 0) < half
    for i in range(0, len(values), 2):
        first, second = values[i], values[min(i + 1, len(values) - 1)]
        for v in range(sizes.vregs):
            one, two = (value[v * SUB : (v + 1) * SUB] for value in (first, second))
            start = 2 * v * sizes.chunk + (index + i) * half
            ref[start : start + SUB, :] = jnp.where(low, one, pltpu.roll(two, half, 0))
            start += sizes.chunk
            ref[start : start + SUB, :] = jnp.where(low, pltpu.roll(one, half, 0), two)


def gather(sizes, ref, index):
    half = SUB // 2
    parts = []
    for part in range(sizes.group):
        start = part * sizes.vec_rows + index * half
        parts.append(ref[start : start + half, :])
    return jnp.concatenate(parts, axis=0)


MOVED = ("state", "source", "mask", "kind", "side")
COUPLING = ("lower", "upper")
MATRICES = ("center", "wall", "flux")


def combine(terms):
    terms = list(terms)
    while len(terms) > 1:
        terms = [
            terms[i] + terms[i + 1] if i + 1 < len(terms) else terms[i]
            for i in range(0, len(terms), 2)
        ]
    return terms[0]


def maps_kernel(sizes, diag_hbm, *refs):
    refs = list(refs)
    take = lambda count: [refs.pop(0) for _ in range(count)]
    sources = take(len(MOVED))
    lower_hbm, upper_hbm, center_hbm, wall_hbm, flux_hbm = take(5)
    out_ref, diag_ref, back_ref, mix_ref, table_ref = take(5)
    targets = take(len(MOVED) + 2)
    fwd_ref, lower_ref, upper_ref, center_ref, wall_ref, flux_ref = take(6)
    plane_sems, sems, scalar_sems = refs
    comps, nx = sizes.comps, sizes.nx
    span = range(comps)
    scalars = [
        pltpu.make_async_copy(source, target, scalar_sems.at[i])
        for i, (source, target) in enumerate(
            (
                (lower_hbm, lower_ref), (upper_hbm, upper_ref), (center_hbm, center_ref),
                (wall_hbm, wall_ref), (flux_hbm, flux_ref),
            )
        )
    ]
    for copy in scalars:
        copy.start()

    def plane_copy(x):
        return pltpu.make_async_copy(diag_hbm.at[x], diag_ref.at[x], plane_sems.at[x])

    for x in range(nx):
        plane_copy(x).start()
    moves = [
        pltpu.make_async_copy(source, target, sems.at[i])
        for i, (source, target) in enumerate(zip(sources + [lower_hbm, upper_hbm], targets))
    ]
    for copy in moves:
        copy.start()
    for copy in scalars:
        copy.wait()

    for c in span:
        for a in span:
            entries = [center_ref[a, c], wall_ref[a, c]] + [flux_ref[a, d, c] for d in range(6)]
            for d, entry in enumerate(entries):
                table_ref[d, c, a] = jnp.full((SUB, LANES), entry, jnp.float32)

    every = slice(None)
    halves = [pl.ds(v * SUB, SUB) for v in range(sizes.vregs)]

    def product(x, half, coupling_ref, negate):
        sign = -1.0 if negate else 1.0
        scale = [[sign * coupling_ref[b, c] for c in span] for b in span]
        rows = []
        for a in span:
            diag = [diag_ref[x, a, b, half] for b in span]
            rows.append([combine(diag[b] * scale[b][c] for b in span) for c in span])
        return rows

    def advance(step, source_ref, source_x, target_ref, target_x, half, added_ref=None):
        for d in span:
            column = [source_ref[source_x, c, d, half] for c in span]
            for a in span:
                value = combine(step[a][c] * column[c] for c in span)
                if added_ref is not None:
                    value = value + added_ref[target_x, a, d, half]
                target_ref[target_x, a, d, half] = value

    plane_copy(0).wait()
    for half in halves:
        first = product(0, half, lower_ref, False)
        for a in span:
            for c in span:
                fwd_ref[0, a, c, half] = first[a][c] * SHRINK

    def forward(x, carry):
        plane_copy(x).wait()
        step = product(x, every, lower_ref, False)
        advance(step, fwd_ref, x - 1, fwd_ref, x, every)
        return carry

    lax.fori_loop(1, nx, forward, 0)

    for half in halves:
        last = product(nx - 1, half, upper_ref, True)
        for a in span:
            for d in span:
                back_ref[nx - 1, a, d, half] = last[a][d]
                mix_ref[nx - 1, a, d, half] = fwd_ref[nx - 1, a, d, half]

    def backward(count, carry):
        x = nx - 1 - count
        for half in halves:
            step = product(x, half, upper_ref, True)
            advance(step, back_ref, x + 1, back_ref, x, half)
            advance(step, mix_ref, x + 1, mix_ref, x, half, fwd_ref)
        return carry

    lax.fori_loop(1, nx, backward, 0)

    pairs = [(a, d) for a in span for d in span]
    scatter(
        sizes, out_ref, sizes.vectors,
        [fwd_ref[nx - 1, a, d] * GROW for a, d in pairs]
        + [back_ref[0, a, d] for a, d in pairs]
        + [mix_ref[0, a, d] for a, d in pairs],
    )
    for copy in moves:
        copy.wait()


def edges_kernel(sizes, gy_two, gz_two, state_ref, mask_ref, *refs):
    masked_ref, inner_ref, outer_ref, *rest = refs
    y_refs = rest[: 1 if gy_two else 2]
    z_refs = rest[len(y_refs) :]
    nx, comps = sizes.nx, sizes.comps
    lane = lax.broadcasted_iota(jnp.int32, (SUB, LANES), 1)
    low_z = (lax.axis_index("gz") == 0).astype(jnp.int32)
    shifts = [low_z] if gz_two else [0, 1]
    packed = [[jnp.zeros((SUB, LANES), jnp.float32)] * (sizes.edge_rows // SUB) for _ in shifts]
    low_y = lax.axis_index("gy") == 0
    even = lax.rem(lax.axis_index("gx"), 2) == 0
    first = []
    for x in range(nx):
        fluid = mask_ref[x].astype(jnp.float32)
        for c in range(comps):
            value = state_ref[x, c] * fluid
            masked_ref[x, c] = value
            if x == 0:
                first.append(value)
            if x == nx - 1:
                inner_ref[c] = jnp.where(even, value, first[c])
                outer_ref[c] = jnp.where(even, first[c], value)
            row = pl.ds(x * comps + c, 1)
            bottom, top = value[0:1], value[sizes.ny - 1 : sizes.ny]
            if gy_two:
                y_refs[0][row, :] = jnp.where(low_y, top, bottom)
            else:
                y_refs[0][row, :] = bottom
                y_refs[1][row, :] = top
            for v in range(sizes.vregs):
                index = (x * comps + c) * sizes.vregs + v
                group, place = divmod(index, LANES)
                part = value[v * SUB : (v + 1) * SUB]
                for side, shift in enumerate(shifts):
                    turned = pltpu.roll(part, lax.rem(jnp.int32(place) + shift, LANES), 1)
                    packed[side][group] = jnp.where(lane == place, turned, packed[side][group])
    for side in range(len(shifts)):
        for group, value in enumerate(packed[side]):
            z_refs[side][group * SUB : (group + 1) * SUB, :] = value


def sweep_steps(sizes, diag_ref, lower_ref, upper_ref):
    span = range(sizes.comps)

    def apply(x, vector):
        return [combine(diag_ref[x, a, b] * vector[b] for b in span) for a in span]

    def coupled(matrix_ref, vector):
        return [combine(matrix_ref[a, b] * vector[b] for b in span) for a in span]

    def forward(x, term, carry):
        pushed = coupled(lower_ref, carry)
        return apply(x, [term[a] + pushed[a] for a in span])

    def backward(x, value, carry):
        pulled = apply(x, coupled(upper_ref, carry))
        return [value[a] - pulled[a] for a in span]

    return forward, backward


def residual_kernel(
    sizes, gy_two, gz_two,
    state_ref, masked_ref, source_ref, mask_ref, kind_ref, side_ref,
    table_ref, diag_ref, lower_ref, upper_ref,
    inner_ref, outer_ref, south_ref, north_ref, below_ref, above_ref, maps_ref,
    residual_hbm, update_ref, out_ref,
    term_ref, swept_ref, zlow_ref, zhigh_ref, west_ref, east_ref, sems,
):
    nx, comps, ny = sizes.nx, sizes.comps, sizes.ny
    span = range(comps)
    shape = (ny, LANES)
    lane = lax.broadcasted_iota(jnp.int32, (SUB, LANES), 1)
    row_index = lax.broadcasted_iota(jnp.int32, shape, 0)
    full_lane = lax.broadcasted_iota(jnp.int32, shape, 1)
    low_y = lax.axis_index("gy") == 0
    low_z = lax.axis_index("gz") == 0
    below, above = below_ref[...], above_ref[...]
    if gz_two:
        below = jnp.where(low_z, 0.0, below)
        above = jnp.where(low_z, above, 0.0)
    zlow_ref[...] = below
    zhigh_ref[...] = above
    even = lax.rem(lax.axis_index("gx"), 2) == 0
    for c in span:
        inner, outer = inner_ref[c], outer_ref[c]
        west_ref[c] = jnp.where(even, outer, inner)
        east_ref[c] = jnp.where(even, inner, outer)
    forward, backward = sweep_steps(sizes, diag_ref, lower_ref, upper_ref)

    def edge_column(ref, x, c, target):
        parts = []
        for v in range(sizes.vregs):
            index = (x * comps + c) * sizes.vregs + v
            group = pl.multiple_of((index >> 7) * SUB, SUB)
            shift = (target - index) & (LANES - 1)
            parts.append(pltpu.roll(ref[pl.ds(group, SUB), :], shift, 1))
        return jnp.concatenate(parts, axis=0)

    def leave(x):
        return pltpu.make_async_copy(term_ref.at[x], residual_hbm.at[x], sems.at[x])

    def plane(x, carry):
        @pl.when(x > 0)
        def send():
            leave(x - 1).start()

        side = side_ref[x]
        fluid = mask_ref[x].astype(jnp.float32)
        kind = kind_ref[x]
        weight = fluid * jnp.where(kind == 0, 1.0, jnp.where(kind == 1, 2.0, 4.0))
        walled = side < 6
        open_face = [side != d for d in range(6)]
        total = [None] * comps

        def add(which, c, value):
            for a in span:
                entry = table_ref[which, c, a]
                term = jnp.concatenate(
                    [entry * value[v * SUB : (v + 1) * SUB] for v in range(sizes.vregs)], axis=0
                )
                total[a] = term if total[a] is None else total[a] + term

        for c in span:
            value = state_ref[x, c]
            add(0, c, value)
            add(1, c, jnp.where(walled, value, 0.0))
            masked = masked_ref[x, c]
            row = pl.ds(x * comps + c, 1)
            south = jnp.broadcast_to(south_ref[row, :], shape)
            north = jnp.broadcast_to(north_ref[row, :], shape)
            if gy_two:
                south = jnp.where(low_y, 0.0, south)
                north = jnp.where(low_y, north, 0.0)
            neighbours = [
                jnp.where(x == 0, west_ref[c], masked_ref[jnp.maximum(x - 1, 0), c]),
                jnp.where(x == nx - 1, east_ref[c], masked_ref[jnp.minimum(x + 1, nx - 1), c]),
                jnp.where(row_index == 0, south, pltpu.roll(masked, 1, 0)),
                jnp.where(row_index == ny - 1, north, pltpu.roll(masked, ny - 1, 0)),
                jnp.where(full_lane == 0, edge_column(zlow_ref, x, c, 0), pltpu.roll(masked, 1, 1)),
                jnp.where(
                    full_lane == LANES - 1,
                    edge_column(zhigh_ref, x, c, LANES - 1),
                    pltpu.roll(masked, LANES - 1, 1),
                ),
            ]
            for d in range(6):
                add(2 + d, c, jnp.where(open_face[d], neighbours[d], 0.0))
        term = [weight * (source_ref[x, a] - total[a]) for a in span]
        for a in span:
            term_ref[x, a] = term[a]
        carry = forward(x, term, carry)
        for a in span:
            swept_ref[x, a] = carry[a]
        return tuple(carry)

    zeroed = tuple(jnp.zeros(shape, jnp.float32) for _ in span)
    ahead = lax.fori_loop(0, nx, plane, zeroed)
    leave(nx - 1).start()

    def back(count, carry):
        x = nx - 1 - count
        carry = backward(x, [swept_ref[x, a] for a in span], carry)
        for a in span:
            update_ref[x, a] = carry[a]
        return tuple(carry)

    behind = lax.fori_loop(0, nx, back, zeroed)
    scatter(sizes, out_ref, 0, list(ahead) + list(behind))
    for x in range(nx):
        leave(x).wait()


def chain(sizes, maps_ref):
    comps, rows, square = sizes.comps, sizes.rows, sizes.square
    span = range(comps)

    def item(part, index):
        start = part * sizes.chunk + index * rows
        return maps_ref[start : start + rows, :]

    def matrix(part, which, vector):
        base = sizes.vectors + which * square
        return [combine(item(part, base + a * comps + b) * vector[b] for b in span) for a in span]

    def ahead(carry):
        entering = []
        for part in range(sizes.group):
            entering.append(carry)
            moved = matrix(part, 0, carry)
            carry = [moved[a] + item(part, a) for a in span]
        return entering, carry

    def behind(carry, ahead_entering):
        entering = []
        for part in reversed(range(sizes.group)):
            entering.insert(0, carry)
            moved = matrix(part, 1, carry)
            mixed = matrix(part, 2, ahead_entering[part])
            carry = [moved[a] + (mixed[a] * GROW + item(part, comps + a)) for a in span]
        return entering, carry

    return ahead, behind


def hop_values(sizes, ref):
    rows = sizes.rows
    return [ref[a * rows : (a + 1) * rows, :] for a in range(sizes.comps)]


def hop_store(sizes, ref, values):
    for a, value in enumerate(values):
        ref[a * sizes.rows : (a + 1) * sizes.rows, :] = value


def ahead_kernel(sizes, entered, maps_ref, *refs):
    *in_refs, out_ref = refs
    zero = [jnp.zeros((sizes.rows, LANES), jnp.float32)] * sizes.comps
    ahead, behind = chain(sizes, maps_ref)
    hop_store(sizes, out_ref, ahead(hop_values(sizes, in_refs[0]) if entered else zero)[1])


def behind_kernel(sizes, entered, last, maps_ref, ahead_ref, *refs):
    *in_refs, out_ref = refs
    zero = [jnp.zeros((sizes.rows, LANES), jnp.float32)] * sizes.comps
    ahead, behind = chain(sizes, maps_ref)
    forward, unused = ahead(hop_values(sizes, ahead_ref) if ahead_ref is not None else zero)
    backward, leaving = behind(hop_values(sizes, in_refs[0]) if entered else zero, forward)
    if not last:
        hop_store(sizes, out_ref, leaving)
        return
    rows = sizes.rows
    for part in range(sizes.group):
        for i, value in enumerate(forward[part] + backward[part]):
            start = part * sizes.vec_rows + i * rows
            out_ref[start : start + rows, :] = value


def put(sizes, ref, first, values):
    rows = sizes.rows
    for i, value in enumerate(values):
        ref[(first + i) * rows : (first + i + 1) * rows, :] = value


def got(sizes, ref, first, count):
    rows = sizes.rows
    return [ref[i * rows : (i + 1) * rows, :] for i in range(first, first + count)]


STEP = 24


def lowered(matrix, power):
    largest = functools.reduce(jnp.maximum, [jnp.abs(entry) for row in matrix for entry in row])
    scale, steps = jnp.ones_like(largest), jnp.zeros_like(largest)
    for i in range(1, 5):
        big = largest > 2.0 ** (STEP * i)
        scale = jnp.where(big, 2.0 ** (-STEP * i), scale)
        steps = jnp.where(big, float(i), steps)
    return [[entry * scale for entry in row] for row in matrix], power + steps


def downscale(steps):
    scale = jnp.ones_like(steps)
    for i in range(1, 6):
        scale = jnp.where(steps >= float(i), 2.0 ** (-STEP * i), scale)
    return scale


def times(left, right):
    span = range(len(left))
    return [[combine(left[a][b] * right[b][c] for b in span) for c in span] for a in span]


def meet_kernel(sizes, maps_ref, out_ref):
    comps, rows, square = sizes.comps, sizes.rows, sizes.square
    span = range(comps)
    zero = jnp.zeros((rows, LANES), jnp.float32)
    ahead, behind = chain(sizes, maps_ref)
    entering, forward = ahead([zero] * comps)
    unused, backward = behind([zero] * comps, entering)

    def matrix(part, which):
        start = part * sizes.chunk + (sizes.vectors + which * square) * rows
        at = lambda i: maps_ref[start + i * rows : start + (i + 1) * rows, :]
        return [[at(a * comps + b) for b in span] for a in span]

    steps, power = [None], zero
    for part in range(sizes.group - 1):
        ahead_map = matrix(part, 0)
        product = ahead_map if part == 0 else times(ahead_map, steps[-1][0])
        steps.append(lowered(product, steps[-1][1] if part else zero))
    total = None
    for part in reversed(range(sizes.group)):
        mixed, mixed_power = lowered(matrix(part, 2), zero + 1.0)
        if part:
            mixed = times(mixed, steps[part][0])
            mixed_power = mixed_power + steps[part][1]
        if total is not None:
            moved, moved_power = lowered(times(matrix(part, 1), total), power)
            highest = jnp.maximum(moved_power, mixed_power)
            one, two = downscale(highest - moved_power), downscale(highest - mixed_power)
            mixed = [[moved[a][b] * one + mixed[a][b] * two for b in span] for a in span]
            mixed_power = highest
        total, power = lowered(mixed, mixed_power)
    left = lax.axis_index("gx") < sizes.group
    put(sizes, out_ref, 0, [jnp.where(left, forward[a], backward[a]) for a in span])
    put(sizes, out_ref, comps, [total[a][b] for a in span for b in span])
    put(sizes, out_ref, comps + square, [power])


def settle_kernel(sizes, maps_ref, own_ref, other_ref, out_ref):
    comps, rows, square = sizes.comps, sizes.rows, sizes.square
    span = range(comps)
    left = lax.axis_index("gx") < sizes.group
    own, other = got(sizes, own_ref, 0, comps), got(sizes, other_ref, 0, comps)
    response = got(sizes, other_ref, comps, square)
    (power,) = got(sizes, other_ref, comps + square, 1)
    mixed = [combine(response[a * comps + b] * own[b] for b in span) for a in span]
    for i in range(12):
        more = power > float(i)
        mixed = [jnp.where(more, value * 2.0**STEP, value) for value in mixed]
    ahead, behind = chain(sizes, maps_ref)
    forward, unused = ahead([jnp.where(left, 0.0, other[a]) for a in span])
    backward, unused = behind([jnp.where(left, other[a] + mixed[a], 0.0) for a in span], forward)
    for part in range(sizes.group):
        for i, value in enumerate(forward[part] + backward[part]):
            start = part * sizes.vec_rows + i * rows
            out_ref[start : start + rows, :] = value


def finish_kernel(sizes, base_ref, back_ref, mix_ref, vec_ref, update_hbm, update_ref, sems):
    comps, nx = sizes.comps, sizes.nx
    span = range(comps)
    ahead = [gather(sizes, vec_ref, a) for a in span]
    behind = [gather(sizes, vec_ref, comps + a) for a in span]

    def leave(x):
        return pltpu.make_async_copy(update_ref.at[x], update_hbm.at[x], sems.at[x])

    def plane(x, carry):
        @pl.when(x > 0)
        def send():
            leave(x - 1).start()

        for a in span:
            mixed = combine(mix_ref[x, a, b] * carry[b] for b in span)
            moved = combine(back_ref[x, a, b] * carry[comps + b] for b in span)
            update_ref[x, a] = base_ref[x, a] + (mixed * GROW + moved)
        return carry

    lax.fori_loop(0, nx, plane, tuple(ahead + behind))
    leave(nx - 1).start()
    for x in range(nx):
        leave(x).wait()


VMEM = pl.BlockSpec(memory_space=pltpu.VMEM)
SMEM = pl.BlockSpec(memory_space=pltpu.SMEM)
HBM = pl.BlockSpec(memory_space=pltpu.HBM)


def floats(shape):
    return jax.ShapeDtypeStruct(shape, jnp.float32)


def call(kernel, name, in_specs, outs, scratch, limit, flops, out_specs=None, aliases=None):
    return pl.pallas_call(
        kernel,
        name=name,
        in_specs=in_specs,
        out_specs=tuple(out_specs or [VMEM] * len(outs)),
        out_shape=tuple(outs),
        scratch_shapes=scratch,
        input_output_aliases=aliases or {},
        compiler_params=pltpu.CompilerParams(vmem_limit_bytes=limit * MIB),
        cost_estimate=pl.CostEstimate(flops=flops, bytes_accessed=1 << 20, transcendentals=0),
    )


def shifted(low, high, axis, count):
    if count == 2:
        other = lax.ppermute(low, axis, [(0, 1), (1, 0)])
        return other, other
    up = [(i, i + 1) for i in range(count - 1)]
    down = [(target, origin) for origin, target in up]
    return lax.ppermute(high, axis, up), lax.ppermute(low, axis, down)


def swapped(inner, outer, count):
    pairs = lambda first: [(i, i + 1) for i in range(first, count - 1, 2)]
    both = lambda first: pairs(first) + [(target, origin) for origin, target in pairs(first)]
    return lax.ppermute(inner, "gx", both(0)), lax.ppermute(outer, "gx", both(1))


def spread(sizes, array, chunk):
    blocks = array.reshape(sizes.group, chunk, LANES)
    groups = [
        list(range(first, first + sizes.group)) for first in range(0, sizes.parts, sizes.group)
    ]
    moved = lax.all_to_all(
        blocks, "gx", split_axis=0, concat_axis=0, tiled=True, axis_index_groups=groups
    )
    return moved.reshape(array.shape)


def solve_pair(sizes, maps):
    count = sizes.comps + sizes.square + 1
    rows = round_up(count * sizes.rows, SUB)
    flops = 1500 * sizes.group * sizes.rows * LANES
    (leaving,) = call(
        functools.partial(meet_kernel, sizes), "meet", [VMEM], [floats((rows, LANES))], [], 4, flops
    )(maps)
    across = [(i, (i + sizes.group) % sizes.parts) for i in range(sizes.parts)]
    arrived = lax.ppermute(leaving, "gx", across)
    (entering,) = call(
        functools.partial(settle_kernel, sizes), "settle", [VMEM] * 3,
        [floats((sizes.group * sizes.vec_rows, LANES))], [], 4, flops,
    )(maps, leaving, arrived)
    return entering


def solve_chain(sizes, maps):
    hop = floats((sizes.hop_rows, LANES))
    up = [(i, i + sizes.group) for i in range(sizes.parts - sizes.group)]
    down = [(target, origin) for origin, target in up]
    flops = 300 * sizes.group * sizes.rows * LANES
    steps = sizes.parts // sizes.group - 1
    ahead = []
    for step in range(steps):
        (leaving,) = call(
            functools.partial(ahead_kernel, sizes, bool(ahead)), "ahead",
            [VMEM] * (1 + len(ahead)), [hop], [], 4, flops,
        )(maps, *ahead)
        ahead = [lax.ppermute(leaving, "gx", up)]
    behind = []
    for step in range(steps + 1):
        last = step == steps
        kernel = functools.partial(behind_kernel, sizes, bool(behind), last)
        if not ahead:
            kernel = functools.partial(
                lambda inner, maps_ref, *refs: inner(maps_ref, None, *refs), kernel
            )
        out = floats((sizes.group * sizes.vec_rows, LANES)) if last else hop
        (leaving,) = call(
            kernel, "behind", [VMEM] * (1 + len(ahead) + len(behind)), [out], [], 4, flops
        )(maps, *ahead, *behind)
        if not last:
            behind = [lax.ppermute(leaving, "gx", down)]
    return leaving


def on_device(
    state_field, source, fluid_mask, cell_kind, boundary_side_number,
    center_matrix, flux_jacobian_blocks, wall_matrix,
    diag_inverse, lower_coupling, upper_neighbour_block,
):
    sizes = Sizes(state_field.shape)
    nx, comps, ny, nz = state_field.shape
    parts = sizes.parts
    gy, gz = lax.axis_size("gy"), lax.axis_size("gz")
    gy_two, gz_two = gy == 2, gz == 2
    square = (nx, comps, comps, ny, nz)
    face = (comps, ny, nz)
    cells = nx * ny * nz
    vmem = lambda shape: pltpu.VMEM(shape, jnp.float32)

    moved = [state_field, source, fluid_mask, cell_kind, boundary_side_number]
    coupling = [lower_coupling, upper_neighbour_block]
    matrices = [center_matrix, wall_matrix, flux_jacobian_blocks.transpose(1, 0, 2)]
    operands = [diag_inverse] + moved + coupling + matrices
    smem = lambda shape: pltpu.SMEM(shape, jnp.float32)
    table = (8, comps, comps, SUB, LANES)
    maps, diag, back, mix, table, *moved = call(
        functools.partial(maps_kernel, sizes), "maps", [HBM] * len(operands),
        [floats((sizes.group * sizes.chunk, LANES)), floats(square), floats(square), floats(square)]
        + [floats(table)]
        + [jax.ShapeDtypeStruct(array.shape, array.dtype) for array in moved + coupling],
        [vmem(square)]
        + [smem(array.shape) for array in coupling + matrices]
        + [
            pltpu.SemaphoreType.DMA((nx,)), pltpu.SemaphoreType.DMA((len(moved + coupling),)),
            pltpu.SemaphoreType.DMA((5,)),
        ],
        24, 1150 * cells,
    )(*(pltpu.with_memory_space_constraint(array, pltpu.HBM) for array in operands))
    state, source, mask, kind, side, lower, upper = moved

    y_count, z_count = (1 if gy_two else 2), (1 if gz_two else 2)
    masked, inner, outer, *rest = call(
        functools.partial(edges_kernel, sizes, gy_two, gz_two), "edges", [VMEM, VMEM],
        [floats(state.shape), floats(face), floats(face)]
        + [floats((nx * comps, nz))] * y_count + [floats((sizes.edge_rows, LANES))] * z_count,
        [], 8, 10 * cells,
    )(state, mask)
    y_low, y_high = rest[0], rest[y_count - 1]
    z_low, z_high = rest[y_count], rest[y_count + z_count - 1]

    from_inner, from_outer = swapped(inner, outer, parts)
    from_south, from_north = shifted(y_low, y_high, "gy", gy)
    from_below, from_above = shifted(z_low, z_high, "gz", gz)

    residual, base, maps = call(
        functools.partial(residual_kernel, sizes, gy_two, gz_two), "residual",
        [VMEM] * 8 + [SMEM] * 2 + [VMEM] * 7,
        [floats(state.shape), floats(state.shape), floats(maps.shape)],
        [
            vmem(state.shape), vmem(state.shape),
            vmem((sizes.edge_rows, LANES)), vmem((sizes.edge_rows, LANES)),
            vmem(face), vmem(face),
            pltpu.SemaphoreType.DMA((nx,)),
        ],
        16, 650 * cells, [HBM, VMEM, VMEM], {16: 2},
    )(
        state, masked, source, mask, kind, side, table, diag, lower, upper,
        from_inner, from_outer, from_south, from_north, from_below, from_above, maps,
    )
    maps = spread(sizes, maps, sizes.chunk)
    solve = solve_pair if parts == 2 * sizes.group else solve_chain
    incoming = spread(sizes, solve(sizes, maps), sizes.vec_rows)
    (update,) = call(
        functools.partial(finish_kernel, sizes), "finish", [VMEM] * 4,
        [floats(state.shape)],
        [vmem(state.shape), pltpu.SemaphoreType.DMA((nx,))],
        16, 200 * cells, [HBM],
    )(base, back, mix, incoming)
    return update, residual


def solution(mesh):
    cells = P("gx", None, "gy", "gz")
    flags = P("gx", "gy", "gz")
    in_specs = (
        cells, cells, flags, flags, flags, P(), P(), P(),
        P("gx", None, None, "gy", "gz"), P(), P(),
    )
    return jax.shard_map(
        on_device, mesh=mesh, in_specs=in_specs, out_specs=(cells, cells), check_vma=False
    )
```
